32 devices in a mesh: dp: 16 (over z, y, core), node: 2 (over x).
Axes of the slice: x: 2, y: 2, z: 4, core: 2. Of those that a mesh axis runs over, the one named last changes fastest.
Arguments:
- node_feats: bfloat16 [768, 25, 128], P(('dp', 'node')), may hold values from -2 to 2
- cotangent: bfloat16 [768, 25, 128], P(('dp', 'node')), may hold values from -3 to 3
- wigner: bfloat16 [13, 25, 8192], P(None, None, ('dp', 'node')), may hold values from -1.25 to 1.25
- radial: bfloat16 [2, 8192, 128], P(None, ('dp', 'node')), may hold values from 0.29882812 to 3
- edge_src: int32 [8192], P(('dp', 'node')), may hold values from 0 to 23
- edge_dst: int32 [8192], P(('dp', 'node')), may hold values from 0 to 23
- edge_count: int32 [32], P(('dp', 'node')), may hold values from 128 to 256
- params: float32 [2, 933888], P(None, ('dp', 'node')), may hold values from -0.5 to 0.5
- moment1: float32 [2, 933888], P(None, ('dp', 'node')), may hold values from -3 to 3
- moment2: float32 [2, 933888], P(None, ('dp', 'node')), may hold values from 1 to 100
Outputs:
- new_params: float32 [2, 933888], P(None, ('dp', 'node'))
- new_moment1: float32 [2, 933888], P(None, ('dp', 'node'))
- new_moment2: float32 [2, 933888], P(None, ('dp', 'node'))
The draws below stay inside these ranges and needn't reach their ends.
Inputs may be any that keep to these rules, and one draw needn't show every extreme that they name: `edge_src`: atom numbers within the edge's own structure. `edge_dst`: atom numbers within the edge's own structure. `edge_count`: slots from this number on within a structure are padding.
All inputs are finite; a program needn't handle non-finite values.
Results may differ from the reference program's by a relative error of at most 0.017.
Values may be sent and summed in bfloat16 or wider, within the bound.
A program may use at most 64 MiB of HBM per device.

```python
import math
import jax
import jax.numpy as jnp
from jax import lax

C = 128
LMAX = 4
LAYERS = 2
NAT = 24
E_DEV = 256
COEF = 25
ROWS = 13
AVG = 10
PARAMS_LAYER = 933888
ATOMS = 768
EDGES = 8192
DEVICES = 32


def plant(result, key, low, top_value):
    longest = result.shape.index(max(result.shape))
    spots = []
    for shift in (0, 1):
        where = [jax.random.randint(jax.random.fold_in(key, axis), (), 0, length) for axis, length in enumerate(result.shape)]
        where[longest] = (where[longest] + shift) % result.shape[longest]
        spots.append(tuple(where))
    return result.at[spots[0]].set(low).at[spots[1]].set(top_value)


def block_scale(own_key, dims, shards, smallest, high):
    def one(position, blocks):
        steps = jax.random.uniform(jax.random.fold_in(jax.random.fold_in(own_key, 6), position), (blocks,), jnp.float32, smallest / len(shards), high / len(shards))
        return jnp.repeat(jnp.exp(steps), dims[position] // blocks).reshape((-1,) + (1,) * (len(dims) - position - 1))

    gain = one(*shards[0])
    for cut in shards[1:]:
        gain = gain * one(*cut)
    return gain


def scatter_about(own_key, dims, width, limit, cuts=(), kind=jnp.bfloat16):
    result = width * jax.random.normal(own_key, dims, jnp.float32)
    if cuts:
        result = result * block_scale(own_key, dims, cuts, -0.22, 0.18)
    return jnp.clip(result, -limit, limit).astype(kind)


def setup_inputs(seed: int = 0) -> dict:
    keys = jax.random.split(jax.random.key(seed), 11)
    node_feats = scatter_about(keys[0], (ATOMS, COEF, C), 0.25, 2.0, ((0, 32),))
    cotangent = scatter_about(keys[1], (ATOMS, COEF, C), 0.5, 3.0, ((0, 32),))
    wigner = scatter_about(keys[2], (ROWS, COEF, EDGES), COEF ** -0.5, 1.25, ((2, 32),))
    radial = jnp.clip(jnp.exp(math.log(3.0) - 2.306499 * jax.random.uniform(keys[3], (LAYERS, EDGES, C), jnp.float32) ** block_scale(keys[3], (LAYERS, EDGES, C), ((1, 32),), -0.2, 0.2)), 0.29882812, 3.0).astype(jnp.bfloat16)
    edge_src = plant(jax.random.randint(keys[4], (EDGES,), 0, NAT), jax.random.fold_in(keys[4], 1), 0, NAT - 1).astype(jnp.int32)
    edge_dst = plant(jax.random.randint(keys[5], (EDGES,), 0, NAT), jax.random.fold_in(keys[5], 1), 0, NAT - 1).astype(jnp.int32)
    edge_count = plant(jax.random.randint(keys[6], (DEVICES,), E_DEV // 2, E_DEV + 1), jax.random.fold_in(keys[6], 1), E_DEV // 2, E_DEV).astype(jnp.int32)
    params = scatter_about(keys[7], (LAYERS, PARAMS_LAYER), ((LMAX + 1) * C // 4) ** -0.5, 0.5, ((1, 32),), jnp.float32)
    moment1 = scatter_about(keys[8], (LAYERS, PARAMS_LAYER), 0.5, 3.0, ((1, 32),), jnp.float32)
    moment2 = jnp.clip(jnp.exp(math.log(100.0) - 4.6051702 * jax.random.uniform(keys[9], (LAYERS, PARAMS_LAYER), jnp.float32) ** block_scale(keys[9], (LAYERS, PARAMS_LAYER), ((1, 32),), -0.2, 0.2)), 1.0, 100.0)
    return dict(node_feats=node_feats, cotangent=cotangent, wigner=wigner, radial=radial, edge_src=edge_src, edge_dst=edge_dst, edge_count=edge_count, params=params, moment1=moment1, moment2=moment2)


def layer(x, flat, wig, rad, src, dst, valid):
    nat, coef, chan = x.shape
    rows = wig.shape[0]
    lone = (rows + 2) // 3
    lmore = lone - 1
    edges = src.shape[0]
    kzero = lone * chan
    kone = lmore * chan
    xs = jnp.take(x, src, axis=0)
    rot = jnp.einsum('kje,ejc->ekc', wig.astype(jnp.float32), xs.astype(jnp.float32))
    rot = (rot * rad.astype(jnp.float32)[:, None, :]).astype(jnp.bfloat16)
    azero = rot[:, :lone].reshape(edges, kzero)
    aplus = rot[:, lone:lone + lmore].reshape(edges, kone)
    aminus = rot[:, lone + lmore:].reshape(edges, kone)
    wzero = flat[:kzero * kzero].reshape(kzero, kzero)
    wreal = flat[kzero * kzero:kzero * kzero + kone * kone].reshape(kone, kone)
    wimag = flat[kzero * kzero + kone * kone:].reshape(kone, kone)
    yzero = jnp.dot(azero, wzero, preferred_element_type=jnp.float32)
    yplus = jnp.dot(aplus, wreal, preferred_element_type=jnp.float32) - jnp.dot(aminus, wimag, preferred_element_type=jnp.float32)
    yminus = jnp.dot(aplus, wimag, preferred_element_type=jnp.float32) + jnp.dot(aminus, wreal, preferred_element_type=jnp.float32)
    mixed = jnp.concatenate([yzero.reshape(edges, lone, chan), yplus.reshape(edges, lmore, chan), yminus.reshape(edges, lmore, chan)], axis=1).astype(jnp.bfloat16)
    message = jnp.einsum('kje,ekc->ejc', wig.astype(jnp.float32), mixed.astype(jnp.float32)) * valid[:, None, None]
    aggregated = jax.ops.segment_sum(message, dst, num_segments=nat) / AVG
    out = x.astype(jnp.float32) + aggregated
    scalar = out[:, 0, :]
    gated = jnp.concatenate([jax.nn.silu(scalar)[:, None, :], out[:, 1:, :] * jax.nn.sigmoid(scalar)[:, None, :]], axis=1)
    return gated.astype(jnp.bfloat16)

def reference(node_feats, cotangent, wigner, radial, edge_src, edge_dst, edge_count, params, moment1, moment2):
    weights = params.astype(jnp.bfloat16)
    feats = node_feats.reshape(DEVICES, NAT, COEF, C)
    cots = cotangent.reshape(DEVICES, NAT, COEF, C)
    wigs = jnp.moveaxis(wigner.reshape(ROWS, COEF, DEVICES, E_DEV), 2, 0)
    rads = jnp.moveaxis(radial.reshape(LAYERS, DEVICES, E_DEV, C), 1, 0)
    sources = edge_src.reshape(DEVICES, E_DEV)
    targets = edge_dst.reshape(DEVICES, E_DEV)

    def structure(carry, item):
        feat, cot, wig, rad, src, dst, count = item
        valid = (jnp.arange(E_DEV, dtype=jnp.int32) < count).astype(jnp.float32)

        def forward(wts):
            hidden = layer(feat, wts[0], wig, rad[0], src, dst, valid)
            return layer(hidden, wts[1], wig, rad[1], src, dst, valid)
        _, pull = jax.vjp(forward, weights)
        grad_dev, = pull(cot)
        return (carry + grad_dev.astype(jnp.float32), None)
    start = jnp.zeros((LAYERS, PARAMS_LAYER), jnp.float32)
    grad, _ = lax.scan(structure, start, (feats, cots, wigs, rads, sources, targets, edge_count))
    new_moment1 = 0.9 * moment1 + 0.1 * grad
    new_moment2 = 0.95 * moment2 + 0.05 * grad * grad
    m_hat = new_moment1 / (1.0 - 0.9 ** 60)
    v_hat = new_moment2 / (1.0 - 0.95 ** 60)
    new_params = params - 0.01 * (m_hat / (jnp.sqrt(v_hat) + 1e-08) + 0.1 * params)
    return (new_params, new_moment1, new_moment2)
```

```python
import functools

import jax
import jax.numpy as jnp
from jax import lax
from jax.experimental import pallas as pl
from jax.experimental.pallas import tpu as pltpu
from jax.sharding import PartitionSpec as P

AVG = 10
LANES = 128
PIECES = 3
LINK = jnp.bfloat16


def split_axes(mesh):
    rest = mesh.shape["dp"] // 2
    y = 1
    while y * y * 4 <= rest and rest % (y * 2) == 0:
        y *= 2
    return rest // y, y, mesh.shape["node"]


def place(dims):
    zs, ys, xs = dims
    dp = lax.axis_index("dp")
    x = lax.axis_index("node")
    core = lax.rem(dp, 2)
    y = lax.rem(dp // 2, ys)
    z = dp // (2 * ys)
    return {"z": z, "y": y, "c": core, "x": x}


def device(dims, at):
    return {"dp": (at["z"] * dims[1] + at["y"]) * 2 + at["c"], "node": at["x"]}


def peer_of(dims, me, axis, step):
    size = {"z": dims[0], "y": dims[1], "c": 2, "x": dims[2]}[axis]
    other = dict(me)
    other[axis] = lax.rem(me[axis] + step, size)
    return other


def size_of(dims, axis):
    return {"z": dims[0], "y": dims[1], "c": 2, "x": dims[2]}[axis]


def greet(dims, me):
    barrier = pltpu.get_barrier_semaphore()
    count = 0
    for axis in "zyxc":
        for step in range(1, size_of(dims, axis)):
            pl.semaphore_signal(
                barrier,
                inc=1,
                device_id=device(dims, peer_of(dims, me, axis, step)),
                device_id_type=pl.DeviceIdType.MESH,
            )
            count += 1
    pl.semaphore_wait(barrier, count)


def gather_kernel(dims, own_ref, out_ref, local_sem, send_sem, recv_sem):
    me = place(dims)
    layers, rows = own_ref.shape[0], own_ref.shape[1]
    part = rows // PIECES
    greet(dims, me)
    mine = pltpu.make_async_copy(
        own_ref, out_ref.at[:, me["z"], me["y"], me["c"], me["x"]], local_sem
    )
    mine.start()

    def view(ref, layer, piece, spans, at):
        index = [layer]
        for axis in "zycx":
            index.append(slice(None) if axis in spans else at[axis])
        index.append(pl.ds(piece * part, part))
        return ref.at[tuple(index)]

    items = []
    for layer in range(layers):
        for piece in range(PIECES):
            order = "zyxc" if (layer * PIECES + piece) % 2 == 0 else "zxyc"
            items.append((layer, piece, order))
    most = max(size_of(dims, a) for a in "zyxc") - 1
    started = []
    for phase in range(4):
        for number, (layer, piece, order) in enumerate(items):
            spans = order[:phase]
            if phase:
                for copy in started[(phase - 1) * len(items) + number]:
                    copy.wait_recv()
            axis = order[phase]
            copies = []
            for step in range(1, size_of(dims, axis)):
                if phase == 0:
                    src = own_ref.at[layer, pl.ds(piece * part, part)]
                else:
                    src = view(out_ref, layer, piece, spans, me)
                slot = (number * 4 + phase) * most + step - 1
                copy = pltpu.make_async_remote_copy(
                    src_ref=src,
                    dst_ref=view(out_ref, layer, piece, spans, me),
                    send_sem=send_sem.at[slot],
                    recv_sem=recv_sem.at[slot],
                    device_id=device(dims, peer_of(dims, me, axis, step)),
                    device_id_type=pl.DeviceIdType.MESH,
                )
                copy.start()
                copies.append(copy)
            started.append(copies)
        if phase == 0:
            mine.wait()
    for copies in started[3 * len(items) :]:
        for copy in copies:
            copy.wait_recv()
    for copies in started:
        for copy in copies:
            copy.wait_send()


def gather_shards(dims, own, collective_id):
    layers, rows, lanes = own.shape
    zs, ys, xs = dims
    most = max(zs, ys, xs, 2) - 1
    slots = layers * PIECES * 4 * most
    return pl.pallas_call(
        functools.partial(gather_kernel, dims),
        out_shape=jax.ShapeDtypeStruct((layers, zs, ys, 2, xs, rows, lanes), own.dtype),
        in_specs=[pl.BlockSpec(memory_space=pltpu.VMEM)],
        out_specs=pl.BlockSpec(memory_space=pltpu.VMEM),
        scratch_shapes=[
            pltpu.SemaphoreType.DMA,
            pltpu.SemaphoreType.DMA((slots,)),
            pltpu.SemaphoreType.DMA((slots,)),
        ],
        compiler_params=pltpu.CompilerParams(
            collective_id=collective_id, has_side_effects=True, vmem_limit_bytes=48 << 20
        ),
        name="gather_shards",
    )(own)


def reduce_buffers(dims, pairs, part):
    zs = dims[0]
    buffers = []
    for first, second, count in pairs:
        n1, n2 = size_of(dims, first), size_of(dims, second)
        buffers += [
            pltpu.VMEM((count, zs, n2, part, LANES), jnp.float32),
            pltpu.VMEM((count, n1 - 1, zs, n2, part, LANES), LINK),
            pltpu.VMEM((count, n1 - 1, zs, n2, part, LANES), LINK),
            pltpu.VMEM((count, zs, part, LANES), jnp.float32),
            pltpu.VMEM((count, n2 - 1, zs, part, LANES), LINK),
            pltpu.VMEM((count, n2 - 1, zs, part, LANES), LINK),
            pltpu.VMEM((count, part, LANES), jnp.float32),
            pltpu.VMEM((count, zs - 1, part, LANES), LINK),
            pltpu.VMEM((count, zs - 1, part, LANES), LINK),
        ]
    return buffers


def reduce_items(layers):
    items = []
    for layer in reversed(range(layers)):
        for piece in range(PIECES):
            number = len(items)
            items.append((layer, piece, number % 2, number // 2))
    return items


def reduce_kernel(dims, grad_ref, out_ref, pair_buf, *scratch):
    zs = dims[0]
    buffers = (scratch[:9], scratch[9:18])
    send_sem, recv_sem = scratch[18:]
    me = place(dims)
    layers, rows = out_ref.shape[0], out_ref.shape[1]
    part = rows // PIECES
    greet(dims, me)
    items = reduce_items(layers)
    most = max(size_of(dims, a) for a in "zyxc") - 1
    pending = []

    def send(number, phase, step, axis, src, dst):
        slot = (number * 4 + phase) * most + step - 1
        copy = pltpu.make_async_remote_copy(
            src_ref=src,
            dst_ref=dst,
            send_sem=send_sem.at[slot],
            recv_sem=recv_sem.at[slot],
            device_id=device(dims, peer_of(dims, me, axis, step)),
            device_id_type=pl.DeviceIdType.MESH,
        )
        copy.start()
        pending.append(copy)
        return copy

    def f32(value):
        return value.astype(jnp.float32)

    waits = {}
    for number, (layer, piece, kind, place_in) in enumerate(items):
        span = pl.ds(piece * part, part)
        waits[number] = [
            send(
                number, 0, 1, "c",
                grad_ref.at[layer, :, :, 1 - me["c"], :, span], pair_buf.at[number],
            )
        ]
    for phase in range(4):
        for number, (layer, piece, kind, place_in) in enumerate(items):
            span = pl.ds(piece * part, part)
            acc1, send1, recv1, acc2, send2, recv2, acc3, send3, recv3 = (
                buf.at[place_in] for buf in buffers[kind]
            )
            first, second = ("x", "y") if kind == 0 else ("y", "x")
            n1, n2 = size_of(dims, first), size_of(dims, second)
            for copy in waits[number]:
                copy.wait_recv()
            copies = []
            if phase == 0:
                for step in list(range(1, n1)) + [0]:
                    k1 = lax.rem(me[first] + step, n1)

                    def one(i, carry, step=step, k1=k1):
                        z, k2 = i // n2, lax.rem(i, n2)
                        y, x = (k2, k1) if kind == 0 else (k1, k2)
                        total = f32(grad_ref[layer, z, y, me["c"], x, span]) + f32(
                            pair_buf[number, z, y, x]
                        )
                        if step:
                            send1[step - 1, z, k2] = total.astype(LINK)
                        else:
                            acc1[z, k2] = total
                        return carry

                    lax.fori_loop(0, zs * n2, one, 0)
                    if step:
                        copies.append(
                            send(number, 1, step, first, send1.at[step - 1], recv1.at[step - 1])
                        )
            elif phase == 1:
                for step in list(range(1, n2)) + [0]:
                    k2 = lax.rem(me[second] + step, n2)

                    def one(z, carry, step=step, k2=k2):
                        total = acc1[z, k2]
                        for e in range(n1 - 1):
                            total = total + f32(recv1[e, z, k2])
                        if step:
                            send2[step - 1, z] = total.astype(LINK)
                        else:
                            acc2[z] = total
                        return carry

                    lax.fori_loop(0, zs, one, 0)
                    if step:
                        copies.append(
                            send(number, 2, step, second, send2.at[step - 1], recv2.at[step - 1])
                        )
            elif phase == 2:
                for step in list(range(1, zs)) + [0]:
                    z = lax.rem(me["z"] + step, zs)
                    total = acc2[z]
                    for e in range(n2 - 1):
                        total = total + f32(recv2[e, z])
                    if step:
                        send3[step - 1] = total.astype(LINK)
                        copies.append(
                            send(number, 3, step, "z", send3.at[step - 1], recv3.at[step - 1])
                        )
                    else:
                        acc3[...] = total
            else:
                total = acc3[...]
                for e in range(zs - 1):
                    total = total + f32(recv3[e])
                out_ref[layer, span] = total
            waits[number] = copies
    for copy in pending:
        copy.wait_send()


def reduce_shards(dims, grad, collective_id):
    layers, zs, ys, _, xs, rows, lanes = grad.shape
    part = rows // PIECES
    most = max(zs, ys, xs, 2) - 1
    count = layers * PIECES
    slots = count * 4 * most
    even, odd = (count + 1) // 2, count // 2
    return pl.pallas_call(
        functools.partial(reduce_kernel, dims),
        out_shape=jax.ShapeDtypeStruct((layers, rows, lanes), jnp.float32),
        in_specs=[pl.BlockSpec(memory_space=pltpu.VMEM)],
        out_specs=pl.BlockSpec(memory_space=pltpu.VMEM),
        scratch_shapes=[pltpu.VMEM((count, zs, ys, xs, part, lanes), grad.dtype)]
        + reduce_buffers(dims, (("x", "y", even), ("y", "x", odd)), part)
        + [pltpu.SemaphoreType.DMA((slots,)), pltpu.SemaphoreType.DMA((slots,))],
        compiler_params=pltpu.CompilerParams(
            collective_id=collective_id, has_side_effects=True, vmem_limit_bytes=48 << 20
        ),
        name="reduce_shards",
    )(grad)


def layer(x, weights, wig, rad, gather, scatter):
    nat, coef, chan = x.shape
    wzero, wreal, wimag = weights
    rows = wig.shape[1]
    lone = (rows + 2) // 3
    lmore = lone - 1
    edges = gather.shape[0]
    kzero, kone = lone * chan, lmore * chan
    xs = jnp.dot(gather, x.reshape(nat, coef * chan), preferred_element_type=jnp.float32)
    xs = xs.astype(jnp.bfloat16).reshape(edges, coef, chan)
    rot = jnp.einsum("ekj,ejc->ekc", wig, xs, preferred_element_type=jnp.float32)
    rot = (rot * rad.astype(jnp.float32)[:, None, :]).astype(jnp.bfloat16)
    azero = rot[:, :lone].reshape(edges, kzero)
    aplus = rot[:, lone : lone + lmore].reshape(edges, kone)
    aminus = rot[:, lone + lmore :].reshape(edges, kone)
    dot = functools.partial(jnp.dot, preferred_element_type=jnp.float32)
    yzero = dot(azero, wzero)
    yplus = dot(aplus, wreal) - dot(aminus, wimag)
    yminus = dot(aplus, wimag) + dot(aminus, wreal)
    mixed = jnp.concatenate([yzero, yplus, yminus], axis=1).astype(jnp.bfloat16)
    mixed = mixed.reshape(edges, rows, chan)
    message = jnp.einsum("ekj,ekc->ejc", wig, mixed, preferred_element_type=jnp.float32)
    summed = jnp.dot(scatter, message.reshape(edges, coef * chan), precision=lax.Precision.HIGH)
    aggregated = summed.reshape(nat, coef, chan) / AVG
    out = x.astype(jnp.float32) + aggregated
    scalar = out[:, 0, :]
    gated = jnp.concatenate(
        [jax.nn.silu(scalar)[:, None, :], out[:, 1:, :] * jax.nn.sigmoid(scalar)[:, None, :]],
        axis=1,
    )
    return gated.astype(jnp.bfloat16)


def local(
    dims, node_feats, cotangent, wigner, radial, edge_src, edge_dst, edge_count, params, moment1,
    moment2,
):
    nat, coef, chan = node_feats.shape
    layers, length = params.shape
    zs, ys, xs = dims
    shards = zs * ys * 2 * xs
    block = LANES * 16 * PIECES
    padded = -(-length // block) * block
    rows = padded // LANES
    own = jnp.pad(params.astype(jnp.bfloat16), ((0, 0), (0, padded - length)))
    full = gather_shards(dims, own.reshape(layers, rows, LANES), 0)
    full = full.reshape(layers, shards, rows, LANES)
    if length % LANES == 0:
        full = full[:, :, : length // LANES]
    else:
        full = full.reshape(layers, shards, padded)[:, :, :length]
    full = full.reshape(layers, shards * length // LANES, LANES)
    lone = (wigner.shape[0] + 2) // 3
    kzero, kone = lone * chan, (lone - 1) * chan
    cut = kzero * kzero // LANES
    step = kone * kone // LANES

    def unpack(flat):
        return (
            flat[:cut].reshape(kzero, kzero),
            flat[cut : cut + step].reshape(kone, kone),
            flat[cut + step :].reshape(kone, kone),
        )

    def pack(grads):
        return jnp.concatenate([g.reshape(-1, LANES) for g in grads], axis=0)

    edges = edge_src.shape[0]
    atoms = jnp.arange(nat, dtype=jnp.int32)
    valid = jnp.arange(edges, dtype=jnp.int32) < edge_count[0]
    gather = (edge_src[:, None] == atoms[None, :]).astype(jnp.bfloat16)
    scatter = jnp.where(valid[None, :], edge_dst[None, :] == atoms[:, None], False)
    scatter = scatter.astype(jnp.float32)
    wig = jnp.transpose(wigner, (2, 0, 1))

    def first(wts):
        return layer(node_feats, wts, wig, radial[0], gather, scatter)

    def second(hidden, wts):
        return layer(hidden, wts, wig, radial[1], gather, scatter)

    hidden, pull_first = jax.vjp(first, unpack(full[0]))
    _, pull_second = jax.vjp(second, hidden, unpack(full[1]))
    back, grad_second = pull_second(cotangent)
    (grad_first,) = pull_first(back)
    grad = jnp.stack([pack(grad_first), pack(grad_second)])
    if length % LANES == 0:
        grad = grad.reshape(layers, shards, length // LANES, LANES)
        grad = jnp.pad(grad, ((0, 0), (0, 0), (0, rows - length // LANES), (0, 0)))
    else:
        grad = grad.reshape(layers, shards, length)
        grad = jnp.pad(grad, ((0, 0), (0, 0), (0, padded - length)))
    owned = reduce_shards(dims, grad.reshape(layers, zs, ys, 2, xs, rows, LANES), 1)
    grad = owned.reshape(layers, padded)[:, :length]
    new_moment1 = 0.9 * moment1 + 0.1 * grad
    new_moment2 = 0.95 * moment2 + 0.05 * grad * grad
    m_hat = new_moment1 / (1.0 - 0.9**60)
    v_hat = new_moment2 / (1.0 - 0.95**60)
    new_params = params - 0.01 * (m_hat / (jnp.sqrt(v_hat) + 1e-08) + 0.1 * params)
    return (new_params, new_moment1, new_moment2)


def solution(mesh):
    both = ("dp", "node")
    return jax.shard_map(
        functools.partial(local, split_axes(mesh)),
        mesh=mesh,
        in_specs=(
            P(both, None, None),
            P(both, None, None),
            P(None, None, both),
            P(None, both, None),
            P(both),
            P(both),
            P(both),
            P(None, both),
            P(None, both),
            P(None, both),
        ),
        out_specs=(P(None, both), P(None, both), P(None, both)),
        check_vma=False,
    )
```

```python
import functools

import jax
import jax.numpy as jnp
from jax import lax
from jax.experimental import pallas as pl
from jax.experimental.pallas import tpu as pltpu
from jax.sharding import PartitionSpec as P

AVG = 10
LANES = 128
PIECES = 3
LINK = jnp.bfloat16


def split_axes(mesh):
    rest = mesh.shape["dp"] // 2
    y = 1
    while y * y * 4 <= rest and rest % (y * 2) == 0:
        y *= 2
    return rest // y, y, mesh.shape["node"]


def place(dims):
    zs, ys, xs = dims
    dp = lax.axis_index("dp")
    x = lax.axis_index("node")
    core = lax.rem(dp, 2)
    y = lax.rem(dp // 2, ys)
    z = dp // (2 * ys)
    return {"z": z, "y": y, "c": core, "x": x}


def device(dims, at):
    return {"dp": (at["z"] * dims[1] + at["y"]) * 2 + at["c"], "node": at["x"]}


def peer_of(dims, me, axis, step):
    size = {"z": dims[0], "y": dims[1], "c": 2, "x": dims[2]}[axis]
    other = dict(me)
    other[axis] = lax.rem(me[axis] + step, size)
    return other


def size_of(dims, axis):
    return {"z": dims[0], "y": dims[1], "c": 2, "x": dims[2]}[axis]


def greet(dims, me):
    barrier = pltpu.get_barrier_semaphore()
    count = 0
    for axis in "zyxc":
        for step in range(1, size_of(dims, axis)):
            pl.semaphore_signal(
                barrier,
                inc=1,
                device_id=device(dims, peer_of(dims, me, axis, step)),
                device_id_type=pl.DeviceIdType.MESH,
            )
            count += 1
    pl.semaphore_wait(barrier, count)


def gather_kernel(dims, own_ref, out_ref, local_sem, send_sem, recv_sem):
    me = place(dims)
    layers, rows = own_ref.shape[0], own_ref.shape[1]
    part = rows // PIECES
    greet(dims, me)
    mine = pltpu.make_async_copy(
        own_ref, out_ref.at[:, me["z"], me["y"], me["c"], me["x"]], local_sem
    )
    mine.start()

    def view(ref, layer, piece, spans, at):
        index = [layer]
        for axis in "zycx":
            index.append(slice(None) if axis in spans else at[axis])
        index.append(pl.ds(piece * part, part))
        return ref.at[tuple(index)]

    items = []
    for layer in range(layers):
        for piece in range(PIECES):
            order = "zyxc" if (layer * PIECES + piece) % 2 == 0 else "zxyc"
            items.append((layer, piece, order))
    most = max(size_of(dims, a) for a in "zyxc") - 1
    started = []
    for phase in range(4):
        for number, (layer, piece, order) in enumerate(items):
            spans = order[:phase]
            if phase:
                for copy in started[(phase - 1) * len(items) + number]:
                    copy.wait_recv()
            axis = order[phase]
            copies = []
            for step in range(1, size_of(dims, axis)):
                if phase == 0:
                    src = own_ref.at[layer, pl.ds(piece * part, part)]
                else:
                    src = view(out_ref, layer, piece, spans, me)
                slot = (number * 4 + phase) * most + step - 1
                copy = pltpu.make_async_remote_copy(
                    src_ref=src,
                    dst_ref=view(out_ref, layer, piece, spans, me),
                    send_sem=send_sem.at[slot],
                    recv_sem=recv_sem.at[slot],
                    device_id=device(dims, peer_of(dims, me, axis, step)),
                    device_id_type=pl.DeviceIdType.MESH,
                )
                copy.start()
                copies.append(copy)
            started.append(copies)
        if phase == 0:
            mine.wait()
    for copies in started[3 * len(items) :]:
        for copy in copies:
            copy.wait_recv()
    for copies in started:
        for copy in copies:
            copy.wait_send()


def gather_shards(dims, own, collective_id):
    layers, rows, lanes = own.shape
    zs, ys, xs = dims
    most = max(zs, ys, xs, 2) - 1
    slots = layers * PIECES * 4 * most
    return pl.pallas_call(
        functools.partial(gather_kernel, dims),
        out_shape=jax.ShapeDtypeStruct((layers, zs, ys, 2, xs, rows, lanes), own.dtype),
        in_specs=[pl.BlockSpec(memory_space=pltpu.VMEM)],
        out_specs=pl.BlockSpec(memory_space=pltpu.VMEM),
        scratch_shapes=[
            pltpu.SemaphoreType.DMA,
            pltpu.SemaphoreType.DMA((slots,)),
            pltpu.SemaphoreType.DMA((slots,)),
        ],
        compiler_params=pltpu.CompilerParams(
            collective_id=collective_id, has_side_effects=True, vmem_limit_bytes=48 << 20
        ),
        name="gather_shards",
    )(own)


def reduce_buffers(dims, pairs, part):
    zs = dims[0]
    buffers = []
    for first, second, count in pairs:
        n1, n2 = size_of(dims, first), size_of(dims, second)
        buffers += [
            pltpu.VMEM((count, zs, n2, part, LANES), jnp.float32),
            pltpu.VMEM((count, n1 - 1, zs, n2, part, LANES), LINK),
            pltpu.VMEM((count, n1 - 1, zs, n2, part, LANES), LINK),
            pltpu.VMEM((count, zs, part, LANES), jnp.float32),
            pltpu.VMEM((count, n2 - 1, zs, part, LANES), LINK),
            pltpu.VMEM((count, n2 - 1, zs, part, LANES), LINK),
            pltpu.VMEM((count, part, LANES), jnp.float32),
            pltpu.VMEM((count, zs - 1, part, LANES), LINK),
            pltpu.VMEM((count, zs - 1, part, LANES), LINK),
        ]
    return buffers


def reduce_items(layers):
    items = []
    for layer in reversed(range(layers)):
        for piece in range(PIECES):
            number = len(items)
            items.append((layer, piece, number % 2, number // 2))
    return items


def reduce_kernel(dims, grad_ref, out_ref, pair_buf, *scratch):
    zs = dims[0]
    buffers = (scratch[:9], scratch[9:18])
    send_sem, recv_sem = scratch[18:]
    me = place(dims)
    layers, rows = out_ref.shape[0], out_ref.shape[1]
    part = rows // PIECES
    greet(dims, me)
    items = reduce_items(layers)
    most = max(size_of(dims, a) for a in "zyxc") - 1
    pending = []

    def send(number, phase, step, axis, src, dst):
        slot = (number * 4 + phase) * most + step - 1
        copy = pltpu.make_async_remote_copy(
            src_ref=src,
            dst_ref=dst,
            send_sem=send_sem.at[slot],
            recv_sem=recv_sem.at[slot],
            device_id=device(dims, peer_of(dims, me, axis, step)),
            device_id_type=pl.DeviceIdType.MESH,
        )
        copy.start()
        pending.append(copy)
        return copy

    def f32(value):
        return value.astype(jnp.float32)

    waits = {}
    for number, (layer, piece, kind, place_in) in enumerate(items):
        span = pl.ds(piece * part, part)
        waits[number] = [
            send(
                number, 0, 1, "c",
                grad_ref.at[layer, :, :, 1 - me["c"], :, span], pair_buf.at[number],
            )
        ]
    for phase in range(4):
        for number, (layer, piece, kind, place_in) in enumerate(items):
            span = pl.ds(piece * part, part)
            acc1, send1, recv1, acc2, send2, recv2, acc3, send3, recv3 = (
                buf.at[place_in] for buf in buffers[kind]
            )
            first, second = ("x", "y") if kind == 0 else ("y", "x")
            n1, n2 = size_of(dims, first), size_of(dims, second)
            for copy in waits[number]:
                copy.wait_recv()
            copies = []
            if phase == 0:
                for step in list(range(1, n1)) + [0]:
                    k1 = lax.rem(me[first] + step, n1)

                    def one(i, carry, step=step, k1=k1):
                        z, k2 = i // n2, lax.rem(i, n2)
                        y, x = (k2, k1) if kind == 0 else (k1, k2)
                        total = f32(grad_ref[layer, z, y, me["c"], x, span]) + f32(
                            pair_buf[number, z, y, x]
                        )
                        if step:
                            send1[step - 1, z, k2] = total.astype(LINK)
                        else:
                            acc1[z, k2] = total
                        return carry

                    lax.fori_loop(0, zs * n2, one, 0)
                    if step:
                        copies.append(
                            send(number, 1, step, first, send1.at[step - 1], recv1.at[step - 1])
                        )
            elif phase == 1:
                for step in list(range(1, n2)) + [0]:
                    k2 = lax.rem(me[second] + step, n2)

                    def one(z, carry, step=step, k2=k2):
                        total = acc1[z, k2]
                        for e in range(n1 - 1):
                            total = total + f32(recv1[e, z, k2])
                        if step:
                            send2[step - 1, z] = total.astype(LINK)
                        else:
                            acc2[z] = total
                        return carry

                    lax.fori_loop(0, zs, one, 0)
                    if step:
                        copies.append(
                            send(number, 2, step, second, send2.at[step - 1], recv2.at[step - 1])
                        )
            elif phase == 2:
                for step in list(range(1, zs)) + [0]:
                    z = lax.rem(me["z"] + step, zs)
                    total = acc2[z]
                    for e in range(n2 - 1):
                        total = total + f32(recv2[e, z])
                    if step:
                        send3[step - 1] = total.astype(LINK)
                        copies.append(
                            send(number, 3, step, "z", send3.at[step - 1], recv3.at[step - 1])
                        )
                    else:
                        acc3[...] = total
            else:
                total = acc3[...]
                for e in range(zs - 1):
                    total = total + f32(recv3[e])
                out_ref[layer, span] = total
            waits[number] = copies
    for copy in pending:
        copy.wait_send()


def reduce_shards(dims, grad, collective_id):
    layers, zs, ys, _, xs, rows, lanes = grad.shape
    part = rows // PIECES
    most = max(zs, ys, xs, 2) - 1
    count = layers * PIECES
    slots = count * 4 * most
    even, odd = (count + 1) // 2, count // 2
    return pl.pallas_call(
        functools.partial(reduce_kernel, dims),
        out_shape=jax.ShapeDtypeStruct((layers, rows, lanes), jnp.float32),
        in_specs=[pl.BlockSpec(memory_space=pltpu.VMEM)],
        out_specs=pl.BlockSpec(memory_space=pltpu.VMEM),
        scratch_shapes=[pltpu.VMEM((count, zs, ys, xs, part, lanes), grad.dtype)]
        + reduce_buffers(dims, (("x", "y", even), ("y", "x", odd)), part)
        + [pltpu.SemaphoreType.DMA((slots,)), pltpu.SemaphoreType.DMA((slots,))],
        compiler_params=pltpu.CompilerParams(
            collective_id=collective_id, has_side_effects=True, vmem_limit_bytes=48 << 20
        ),
        name="reduce_shards",
    )(grad)


def mix(source, wig, outputs, inputs, coef, transposed, chan, edges, write):
    tall = 16
    wide = LANES if edges % LANES == 0 else edges
    across = edges // wide

    def one(number, carry):
        t, h = number // across, lax.rem(number, across)
        cols = pl.ds(pl.multiple_of(h * wide, wide), wide)
        tiles = [
            source[pl.ds(pl.multiple_of(i * chan + t * tall, tall), tall), cols]
            for i in range(inputs)
        ]
        for o in range(outputs):
            total = None
            for i in range(inputs):
                row = i * coef + o if transposed else o * coef + i
                term = wig[pl.ds(row, 1), cols] * tiles[i]
                total = term if total is None else total + term
            write(o, pl.multiple_of(t * tall, tall), cols, total)
        return carry

    lax.fori_loop(0, (chan // tall) * across, one, 0)


def dot(a, b, over=(1, 0)):
    return lax.dot_general(
        a, b, (((over[0],), (over[1],)), ((), ())), preferred_element_type=jnp.float32
    )


def compute_kernel(
    shape, count_ref, x_ref, cot_ref, wig_ref, rad_ref, src_ref, dst_ref, flat_ref, grad_ref,
    rows_f, wzero, wreal, wimag, edge_f, edge_g, rotated, small_f, outs, hidden, back, dnode, dmix,
):
    nat, coef, chan, rows, edges = shape
    lone = (rows + 2) // 3
    kzero, kone = lone * chan, (lone - 1) * chan
    atoms = lax.broadcasted_iota(jnp.int32, (nat, edges), 0)
    slots = lax.broadcasted_iota(jnp.int32, (nat, edges), 1)
    take = (src_ref[...] == atoms).astype(jnp.float32).astype(jnp.bfloat16)
    live = (dst_ref[...] == atoms) & (slots < count_ref[0])
    put = live.astype(jnp.float32).astype(jnp.bfloat16)

    def per_coef(body):
        def one(j, carry):
            body(pl.ds(pl.multiple_of(j * chan, chan), chan))
            return carry

        lax.fori_loop(0, coef, one, 0)

    def blocks():
        cut = kzero * kzero // LANES
        step = kone * kone // LANES
        return ((wzero, 0, kzero), (wreal, cut, kone), (wimag, cut + step, kone))

    def load_weights(layer):
        rows_f[...] = flat_ref[layer].astype(jnp.float32)
        for ref, start, size in blocks():
            per = size // LANES
            for c in range(per):
                ref[:, c * LANES : (c + 1) * LANES] = rows_f[
                    pl.ds(start + c, size, stride=per), :
                ].astype(jnp.bfloat16)

    def store_grads(layer, grads):
        for (_, start, size), grad in zip(blocks(), grads):
            per = size // LANES
            value = grad()
            for c in range(per):
                rows_f[pl.ds(start + c, size, stride=per), :] = value[
                    :, c * LANES : (c + 1) * LANES
                ]
        grad_ref[layer] = rows_f[...].astype(jnp.bfloat16)

    def forward(layer, node, last):
        def pick(at):
            edge_f[at, :] = dot(node[at, :], take)

        per_coef(pick)

        def write(o, t, cols, total):
            scaled = total * rad_ref[layer, pl.ds(t, 16), cols].astype(jnp.float32)
            rotated[layer, pl.ds(o * chan + t, 16), cols] = scaled.astype(jnp.bfloat16)

        mix(edge_f, wig_ref, rows, coef, coef, False, chan, edges, write)
        azero = rotated[layer, :kzero]
        aplus = rotated[layer, kzero : kzero + kone]
        aminus = rotated[layer, kzero + kone :]

        def rounded(value):
            return value.astype(jnp.bfloat16).astype(jnp.float32)

        small_f[:kzero] = rounded(dot(wzero[...], azero, (0, 0)))
        small_f[kzero : kzero + kone] = rounded(
            dot(wreal[...], aplus, (0, 0)) - dot(wimag[...], aminus, (0, 0))
        )
        small_f[kzero + kone :] = rounded(
            dot(wimag[...], aplus, (0, 0)) + dot(wreal[...], aminus, (0, 0))
        )

        def message(o, t, cols, total):
            edge_g[pl.ds(o * chan + t, 16), cols] = total

        mix(small_f, wig_ref, coef, rows, coef, True, chan, edges, message)

        def gathered(at):
            value = edge_g[at, :]
            high = value.astype(jnp.bfloat16)
            low = (value - high.astype(jnp.float32)).astype(jnp.bfloat16)
            total = dot(high, put, (1, 1)) + dot(low, put, (1, 1))
            outs[layer, at, :] = node[at, :].astype(jnp.float32) + total / AVG

        per_coef(gathered)
        if last:
            return
        gate = jax.nn.sigmoid(outs[layer, :chan, :])

        def activate(at):
            hidden[at, :] = (outs[layer, at, :] * gate).astype(jnp.bfloat16)

        per_coef(activate)

    def backward(layer, cot, last):
        scalar = outs[layer, :chan, :]
        gate = jax.nn.sigmoid(scalar)
        slope = gate * (1.0 - gate)

        def one(j, total):
            at = pl.ds(pl.multiple_of(j * chan, chan), chan)
            value = cot[at, :].astype(jnp.float32)
            dnode[at, :] = value * gate
            return total + value * outs[layer, at, :]

        total = lax.fori_loop(1, coef, one, jnp.zeros((chan, nat), jnp.float32))
        lead = cot[:chan, :].astype(jnp.float32)
        dnode[:chan, :] = lead * (gate + scalar * slope) + total * slope

        def spread(at):
            value = dnode[at, :] / AVG
            high = value.astype(jnp.bfloat16)
            low = (value - high.astype(jnp.float32)).astype(jnp.bfloat16)
            edge_f[at, :] = dot(high, put) + dot(low, put)

        per_coef(spread)

        def write(o, t, cols, total):
            dmix[pl.ds(o * chan + t, 16), cols] = total.astype(jnp.bfloat16)

        mix(edge_f, wig_ref, rows, coef, coef, False, chan, edges, write)
        dzero = dmix[:kzero]
        dplus = dmix[kzero : kzero + kone]
        dminus = dmix[kzero + kone :]
        azero = rotated[layer, :kzero]
        aplus = rotated[layer, kzero : kzero + kone]
        aminus = rotated[layer, kzero + kone :]
        store_grads(
            layer,
            (
                lambda: dot(azero, dzero, (1, 1)),
                lambda: dot(aplus, dplus, (1, 1)) + dot(aminus, dminus, (1, 1)),
                lambda: dot(aplus, dminus, (1, 1)) - dot(aminus, dplus, (1, 1)),
            ),
        )
        if last:
            return

        def scaled(value):
            value = value.astype(jnp.bfloat16).astype(jnp.float32)
            scale = rad_ref[layer].astype(jnp.float32)
            parts = value.shape[0] // chan
            return jnp.concatenate(
                [value[k * chan : (k + 1) * chan] * scale for k in range(parts)], axis=0
            )

        small_f[:kzero] = scaled(dot(wzero[...], dzero))
        small_f[kzero : kzero + kone] = scaled(
            dot(wreal[...], dplus) + dot(wimag[...], dminus)
        )
        small_f[kzero + kone :] = scaled(dot(wreal[...], dminus) - dot(wimag[...], dplus))

        def spill(o, t, cols, total):
            edge_g[pl.ds(o * chan + t, 16), cols] = total

        mix(small_f, wig_ref, coef, rows, coef, True, chan, edges, spill)

        def collect(at):
            value = edge_g[at, :].astype(jnp.bfloat16)
            back[at, :] = (dnode[at, :] + dot(value, take, (1, 1))).astype(jnp.bfloat16)

        per_coef(collect)

    load_weights(0)
    forward(0, x_ref, False)
    load_weights(1)
    forward(1, hidden, True)
    backward(1, cot_ref, False)
    backward(0, back, True)


def device_grads(count, feats, cot, wig, rad, src, dst, flat, shape):
    nat, coef, chan, rows, edges = shape
    lone = (rows + 2) // 3
    kzero, kone = lone * chan, (lone - 1) * chan
    wide = coef * chan
    vmem = pl.BlockSpec(memory_space=pltpu.VMEM)
    return pl.pallas_call(
        functools.partial(compute_kernel, shape),
        out_shape=jax.ShapeDtypeStruct(flat.shape, jnp.bfloat16),
        in_specs=[pl.BlockSpec(memory_space=pltpu.SMEM)] + [vmem] * 7,
        out_specs=vmem,
        scratch_shapes=[
            pltpu.VMEM(flat.shape[1:], jnp.float32),
            pltpu.VMEM((kzero, kzero), jnp.bfloat16),
            pltpu.VMEM((kone, kone), jnp.bfloat16),
            pltpu.VMEM((kone, kone), jnp.bfloat16),
            pltpu.VMEM((wide, edges), jnp.float32),
            pltpu.VMEM((wide, edges), jnp.float32),
            pltpu.VMEM((2, rows * chan, edges), jnp.bfloat16),
            pltpu.VMEM((rows * chan, edges), jnp.float32),
            pltpu.VMEM((2, wide, nat), jnp.float32),
            pltpu.VMEM((wide, nat), jnp.bfloat16),
            pltpu.VMEM((wide, nat), jnp.bfloat16),
            pltpu.VMEM((wide, nat), jnp.float32),
            pltpu.VMEM((rows * chan, edges), jnp.bfloat16),
        ],
        compiler_params=pltpu.CompilerParams(vmem_limit_bytes=56 << 20),
        name="device_grads",
    )(count, feats, cot, wig, rad, src, dst, flat)


def local(
    dims, node_feats, cotangent, wigner, radial, edge_src, edge_dst, edge_count, params, moment1,
    moment2,
):
    nat, coef, chan = node_feats.shape
    layers, length = params.shape
    zs, ys, xs = dims
    shards = zs * ys * 2 * xs
    block = LANES * 16 * PIECES
    padded = -(-length // block) * block
    rows = padded // LANES
    own = jnp.pad(params.astype(jnp.bfloat16), ((0, 0), (0, padded - length)))
    full = gather_shards(dims, own.reshape(layers, rows, LANES), 0)
    full = full.reshape(layers, shards, rows, LANES)
    if length % LANES == 0:
        full = full[:, :, : length // LANES]
    else:
        full = full.reshape(layers, shards, padded)[:, :, :length]
    full = full.reshape(layers, shards * length // LANES, LANES)
    edges = edge_src.shape[0]

    def turned(nodes):
        return jnp.transpose(nodes.reshape(nat, coef * chan))

    grad = device_grads(
        edge_count,
        turned(node_feats),
        turned(cotangent),
        wigner.reshape(-1, edges).astype(jnp.float32),
        jnp.transpose(radial, (0, 2, 1)),
        edge_src[None, :],
        edge_dst[None, :],
        full,
        (nat, coef, chan, wigner.shape[0], edges),
    )
    if length % LANES == 0:
        grad = grad.reshape(layers, shards, length // LANES, LANES)
        grad = jnp.pad(grad, ((0, 0), (0, 0), (0, rows - length // LANES), (0, 0)))
    else:
        grad = grad.reshape(layers, shards, length)
        grad = jnp.pad(grad, ((0, 0), (0, 0), (0, padded - length)))
    owned = reduce_shards(dims, grad.reshape(layers, zs, ys, 2, xs, rows, LANES), 1)
    grad = owned.reshape(layers, padded)[:, :length]
    new_moment1 = 0.9 * moment1 + 0.1 * grad
    new_moment2 = 0.95 * moment2 + 0.05 * grad * grad
    m_hat = new_moment1 / (1.0 - 0.9**60)
    v_hat = new_moment2 / (1.0 - 0.95**60)
    new_params = params - 0.01 * (m_hat / (jnp.sqrt(v_hat) + 1e-08) + 0.1 * params)
    return (new_params, new_moment1, new_moment2)


def solution(mesh):
    both = ("dp", "node")
    return jax.shard_map(
        functools.partial(local, split_axes(mesh)),
        mesh=mesh,
        in_specs=(
            P(both, None, None),
            P(both, None, None),
            P(None, None, both),
            P(None, both, None),
            P(both),
            P(both),
            P(both),
            P(None, both),
            P(None, both),
            P(None, both),
        ),
        out_specs=(P(None, both), P(None, both), P(None, both)),
        check_vma=False,
    )
```

```python
import functools

import jax
import jax.numpy as jnp
from jax import lax
from jax.experimental import pallas as pl
from jax.experimental.pallas import tpu as pltpu
from jax.sharding import PartitionSpec as P

AVG = 10
LANES = 128
PIECES = 3
LINK = jnp.bfloat16


def split_axes(mesh):
    rest = mesh.shape["dp"] // 2
    y = 1
    while y * y * 4 <= rest and rest % (y * 2) == 0:
        y *= 2
    return rest // y, y, mesh.shape["node"]


def place(dims):
    zs, ys, xs = dims
    dp = lax.axis_index("dp")
    x = lax.axis_index("node")
    core = lax.rem(dp, 2)
    y = lax.rem(dp // 2, ys)
    z = dp // (2 * ys)
    return {"z": z, "y": y, "c": core, "x": x}


def device(dims, at):
    return {"dp": (at["z"] * dims[1] + at["y"]) * 2 + at["c"], "node": at["x"]}


def peer_of(dims, me, axis, step):
    size = {"z": dims[0], "y": dims[1], "c": 2, "x": dims[2]}[axis]
    other = dict(me)
    other[axis] = lax.rem(me[axis] + step, size)
    return other


def size_of(dims, axis):
    return {"z": dims[0], "y": dims[1], "c": 2, "x": dims[2]}[axis]


def greet(dims, me):
    barrier = pltpu.get_barrier_semaphore()
    count = 0
    for axis in "zyxc":
        for step in range(1, size_of(dims, axis)):
            pl.semaphore_signal(
                barrier,
                inc=1,
                device_id=device(dims, peer_of(dims, me, axis, step)),
                device_id_type=pl.DeviceIdType.MESH,
            )
            count += 1
    pl.semaphore_wait(barrier, count)


def gather_steps(dims, me, own_ref, out_ref, local_sem, send_sem, recv_sem):
    layers, rows = own_ref.shape[0], own_ref.shape[1]
    part = rows // PIECES
    mine = pltpu.make_async_copy(
        own_ref, out_ref.at[:, me["z"], me["y"], me["c"], me["x"]], local_sem
    )
    mine.start()
    most = max(size_of(dims, a) for a in "zyxc") - 1
    started = {}
    state = {"mine": True}

    def view(ref, layer, piece, spans, at):
        index = [layer]
        for axis in "zycx":
            index.append(slice(None) if axis in spans else at[axis])
        index.append(pl.ds(piece * part, part))
        return ref.at[tuple(index)]

    def advance(layer, phase):
        for piece in range(PIECES):
            number = layer * PIECES + piece
            order = "zyxc" if number % 2 == 0 else "zxyc"
            if phase:
                for copy in started[number, phase - 1]:
                    copy.wait_recv()
                if state["mine"]:
                    mine.wait()
                    state["mine"] = False
            if phase == 4:
                continue
            axis, spans = order[phase], order[:phase]
            copies = []
            for step in range(1, size_of(dims, axis)):
                if phase == 0:
                    src = own_ref.at[layer, pl.ds(piece * part, part)]
                else:
                    src = view(out_ref, layer, piece, spans, me)
                slot = (number * 4 + phase) * most + step - 1
                copy = pltpu.make_async_remote_copy(
                    src_ref=src,
                    dst_ref=view(out_ref, layer, piece, spans, me),
                    send_sem=send_sem.at[slot],
                    recv_sem=recv_sem.at[slot],
                    device_id=device(dims, peer_of(dims, me, axis, step)),
                    device_id_type=pl.DeviceIdType.MESH,
                )
                copy.start()
                copies.append(copy)
            started[number, phase] = copies

    def finish():
        for copies in started.values():
            for copy in copies:
                copy.wait_send()

    return advance, finish


def gather_kernel(dims, own_ref, out_ref, local_sem, send_sem, recv_sem):
    me = place(dims)
    greet(dims, me)
    advance, finish = gather_steps(dims, me, own_ref, out_ref, local_sem, send_sem, recv_sem)
    for phase in range(5):
        for layer in range(own_ref.shape[0]):
            advance(layer, phase)
    finish()


def gather_shards(dims, own, collective_id):
    layers, rows, lanes = own.shape
    zs, ys, xs = dims
    most = max(zs, ys, xs, 2) - 1
    slots = layers * PIECES * 4 * most
    return pl.pallas_call(
        functools.partial(gather_kernel, dims),
        out_shape=jax.ShapeDtypeStruct((layers, zs, ys, 2, xs, rows, lanes), own.dtype),
        in_specs=[pl.BlockSpec(memory_space=pltpu.VMEM)],
        out_specs=pl.BlockSpec(memory_space=pltpu.VMEM),
        scratch_shapes=[
            pltpu.SemaphoreType.DMA,
            pltpu.SemaphoreType.DMA((slots,)),
            pltpu.SemaphoreType.DMA((slots,)),
        ],
        compiler_params=pltpu.CompilerParams(
            collective_id=collective_id, has_side_effects=True, vmem_limit_bytes=48 << 20
        ),
        name="gather_shards",
    )(own)


def reduce_buffers(dims, pairs, part):
    zs = dims[0]
    buffers = []
    for first, second, count in pairs:
        n1, n2 = size_of(dims, first), size_of(dims, second)
        buffers += [
            pltpu.VMEM((count, zs, n2, part, LANES), jnp.float32),
            pltpu.VMEM((count, n1 - 1, zs, n2, part, LANES), LINK),
            pltpu.VMEM((count, n1 - 1, zs, n2, part, LANES), LINK),
            pltpu.VMEM((count, zs, part, LANES), jnp.float32),
            pltpu.VMEM((count, n2 - 1, zs, part, LANES), LINK),
            pltpu.VMEM((count, n2 - 1, zs, part, LANES), LINK),
            pltpu.VMEM((count, part, LANES), jnp.float32),
            pltpu.VMEM((count, zs - 1, part, LANES), LINK),
            pltpu.VMEM((count, zs - 1, part, LANES), LINK),
        ]
    return buffers


def reduce_items(layers):
    items = []
    for layer in reversed(range(layers)):
        for piece in range(PIECES):
            number = len(items)
            items.append((layer, piece, number % 2, number // 2))
    return items


def reduce_steps(dims, me, grad_ref, out_ref, pair_buf, scratch):
    zs = dims[0]
    buffers = (scratch[:9], scratch[9:18])
    send_sem, recv_sem = scratch[18:20]
    layers, rows = out_ref.shape[0], out_ref.shape[1]
    part = rows // PIECES
    items = reduce_items(layers)
    most = max(size_of(dims, a) for a in "zyxc") - 1
    pending = []

    def send(number, phase, step, axis, src, dst):
        slot = (number * 4 + phase) * most + step - 1
        copy = pltpu.make_async_remote_copy(
            src_ref=src,
            dst_ref=dst,
            send_sem=send_sem.at[slot],
            recv_sem=recv_sem.at[slot],
            device_id=device(dims, peer_of(dims, me, axis, step)),
            device_id_type=pl.DeviceIdType.MESH,
        )
        copy.start()
        pending.append(copy)
        return copy

    def f32(value):
        return value.astype(jnp.float32)

    waits = {}

    def advance(wanted, now):
        phase = now - 1
        for number, (layer, piece, kind, place_in) in enumerate(items):
            if layer != wanted:
                continue
            if now == 0:
                waits[number] = [
                    send(
                        number, 0, 1, "c",
                        grad_ref.at[layer, :, :, 1 - me["c"], :, pl.ds(piece * part, part)],
                        pair_buf.at[number],
                    )
                ]
                continue
            span = pl.ds(piece * part, part)
            acc1, send1, recv1, acc2, send2, recv2, acc3, send3, recv3 = (
                buf.at[place_in] for buf in buffers[kind]
            )
            first, second = ("x", "y") if kind == 0 else ("y", "x")
            n1, n2 = size_of(dims, first), size_of(dims, second)
            for copy in waits[number]:
                copy.wait_recv()
            copies = []
            if phase == 0:
                for step in list(range(1, n1)) + [0]:
                    k1 = lax.rem(me[first] + step, n1)

                    def one(i, carry, step=step, k1=k1):
                        z, k2 = i // n2, lax.rem(i, n2)
                        y, x = (k2, k1) if kind == 0 else (k1, k2)
                        total = f32(grad_ref[layer, z, y, me["c"], x, span]) + f32(
                            pair_buf[number, z, y, x]
                        )
                        if step:
                            send1[step - 1, z, k2] = total.astype(LINK)
                        else:
                            acc1[z, k2] = total
                        return carry

                    lax.fori_loop(0, zs * n2, one, 0)
                    if step:
                        copies.append(
                            send(number, 1, step, first, send1.at[step - 1], recv1.at[step - 1])
                        )
            elif phase == 1:
                for step in list(range(1, n2)) + [0]:
                    k2 = lax.rem(me[second] + step, n2)

                    def one(z, carry, step=step, k2=k2):
                        total = acc1[z, k2]
                        for e in range(n1 - 1):
                            total = total + f32(recv1[e, z, k2])
                        if step:
                            send2[step - 1, z] = total.astype(LINK)
                        else:
                            acc2[z] = total
                        return carry

                    lax.fori_loop(0, zs, one, 0)
                    if step:
                        copies.append(
                            send(number, 2, step, second, send2.at[step - 1], recv2.at[step - 1])
                        )
            elif phase == 2:
                for step in list(range(1, zs)) + [0]:
                    z = lax.rem(me["z"] + step, zs)
                    total = acc2[z]
                    for e in range(n2 - 1):
                        total = total + f32(recv2[e, z])
                    if step:
                        send3[step - 1] = total.astype(LINK)
                        copies.append(
                            send(number, 3, step, "z", send3.at[step - 1], recv3.at[step - 1])
                        )
                    else:
                        acc3[...] = total
            else:
                total = acc3[...]
                for e in range(zs - 1):
                    total = total + f32(recv3[e])
                out_ref[layer, span] = total
            waits[number] = copies

    def finish():
        for copy in pending:
            copy.wait_send()

    return advance, finish


def reduce_kernel(dims, grad_ref, out_ref, pair_buf, *scratch):
    me = place(dims)
    greet(dims, me)
    advance, finish = reduce_steps(dims, me, grad_ref, out_ref, pair_buf, scratch)
    for phase in range(5):
        for layer in reversed(range(out_ref.shape[0])):
            advance(layer, phase)
    finish()


def reduce_shards(dims, grad, collective_id):
    layers, _, _, _, _, rows, lanes = grad.shape
    return pl.pallas_call(
        functools.partial(reduce_kernel, dims),
        out_shape=jax.ShapeDtypeStruct((layers, rows, lanes), jnp.float32),
        in_specs=[pl.BlockSpec(memory_space=pltpu.VMEM)],
        out_specs=pl.BlockSpec(memory_space=pltpu.VMEM),
        scratch_shapes=reduce_scratch(dims, layers, rows),
        compiler_params=pltpu.CompilerParams(
            collective_id=collective_id, has_side_effects=True, vmem_limit_bytes=48 << 20
        ),
        name="reduce_shards",
    )(grad)


def mix(source, wig, outputs, inputs, coef, transposed, chan, edges, write, hooks=()):
    tall = 16
    wide = LANES if edges % LANES == 0 else edges
    across = edges // wide

    def one(number, carry):
        t, h = number // across, lax.rem(number, across)
        cols = pl.ds(pl.multiple_of(h * wide, wide), wide)
        tiles = [
            source[pl.ds(pl.multiple_of(i * chan + t * tall, tall), tall), cols]
            for i in range(inputs)
        ]
        for o in range(outputs):
            total = None
            for i in range(inputs):
                row = i * coef + o if transposed else o * coef + i
                term = wig[pl.ds(row, 1), cols] * tiles[i]
                total = term if total is None else total + term
            write(o, pl.multiple_of(t * tall, tall), cols, total)
        return carry

    total = (chan // tall) * across
    spans = len(hooks) + 1
    for n in range(spans):
        lax.fori_loop(n * total // spans, (n + 1) * total // spans, one, 0)
        if n < len(hooks):
            hooks[n]()


def dot(a, b, over=(1, 0)):
    return lax.dot_general(
        a, b, (((over[0],), (over[1],)), ((), ())), preferred_element_type=jnp.float32
    )


def compute_kernel(
    shape, count_ref, x_ref, cot_ref, wig_ref, rad_ref, src_ref, dst_ref, flat_ref, grad_ref,
    *scratch,
):
    rows_f = scratch[0]

    def unpack(layer):
        rows_f[...] = flat_ref[layer].astype(jnp.float32)

    def pack(layer):
        grad_ref[layer] = rows_f[...].astype(jnp.bfloat16)

    refs = (count_ref, x_ref, cot_ref, wig_ref, rad_ref, src_ref, dst_ref)
    compute(shape, refs, scratch, unpack, pack, lambda *step: None, lambda *step: None)


def compute(shape, refs, scratch, unpack, pack, gather, reduce):
    count_ref, x_ref, cot_ref, wig_ref, rad_ref, src_ref, dst_ref = refs
    (rows_f, wzero, wreal, wimag, edge_f, edge_g, rotated, small_f, outs, hidden, back, dnode, dmix) = scratch
    nat, coef, chan, rows, edges = shape
    lone = (rows + 2) // 3
    kzero, kone = lone * chan, (lone - 1) * chan
    atoms = lax.broadcasted_iota(jnp.int32, (nat, edges), 0)
    slots = lax.broadcasted_iota(jnp.int32, (nat, edges), 1)
    take = (src_ref[...] == atoms).astype(jnp.float32).astype(jnp.bfloat16)
    live = (dst_ref[...] == atoms) & (slots < count_ref[0])
    put = live.astype(jnp.float32).astype(jnp.bfloat16)

    def per_coef(body):
        def one(j, carry):
            body(pl.ds(pl.multiple_of(j * chan, chan), chan))
            return carry

        lax.fori_loop(0, coef, one, 0)

    def blocks():
        cut = kzero * kzero // LANES
        step = kone * kone // LANES
        return ((wzero, 0, kzero), (wreal, cut, kone), (wimag, cut + step, kone))

    def load_weights(layer):
        unpack(layer)
        for ref, start, size in blocks():
            per = size // LANES
            for c in range(per):
                ref[:, c * LANES : (c + 1) * LANES] = rows_f[
                    pl.ds(start + c, size, stride=per), :
                ].astype(jnp.bfloat16)

    def store_grads(layer, grads):
        for (_, start, size), grad in zip(blocks(), grads):
            per = size // LANES
            value = grad()
            for c in range(per):
                rows_f[pl.ds(start + c, size, stride=per), :] = value[
                    :, c * LANES : (c + 1) * LANES
                ]
        pack(layer)

    def forward(layer, node, last, early, late):
        def pick(at):
            edge_f[at, :] = dot(node[at, :], take)

        per_coef(pick)

        def write(o, t, cols, total):
            scaled = total * rad_ref[layer, pl.ds(t, 16), cols].astype(jnp.float32)
            rotated[layer, pl.ds(o * chan + t, 16), cols] = scaled.astype(jnp.bfloat16)

        mix(edge_f, wig_ref, rows, coef, coef, False, chan, edges, write, early)
        gather(layer, 4)
        load_weights(layer)
        azero = rotated[layer, :kzero]
        aplus = rotated[layer, kzero : kzero + kone]
        aminus = rotated[layer, kzero + kone :]

        def rounded(value):
            return value.astype(jnp.bfloat16).astype(jnp.float32)

        small_f[:kzero] = rounded(dot(wzero[...], azero, (0, 0)))
        small_f[kzero : kzero + kone] = rounded(
            dot(wreal[...], aplus, (0, 0)) - dot(wimag[...], aminus, (0, 0))
        )
        small_f[kzero + kone :] = rounded(
            dot(wimag[...], aplus, (0, 0)) + dot(wreal[...], aminus, (0, 0))
        )

        def message(o, t, cols, total):
            edge_g[pl.ds(o * chan + t, 16), cols] = total

        mix(small_f, wig_ref, coef, rows, coef, True, chan, edges, message, late)

        def gathered(at):
            value = edge_g[at, :]
            high = value.astype(jnp.bfloat16)
            low = (value - high.astype(jnp.float32)).astype(jnp.bfloat16)
            total = dot(high, put, (1, 1)) + dot(low, put, (1, 1))
            outs[layer, at, :] = node[at, :].astype(jnp.float32) + total / AVG

        per_coef(gathered)
        if last:
            return
        gate = jax.nn.sigmoid(outs[layer, :chan, :])

        def activate(at):
            hidden[at, :] = (outs[layer, at, :] * gate).astype(jnp.bfloat16)

        per_coef(activate)

    def backward(layer, cot, last, early, late):
        scalar = outs[layer, :chan, :]
        gate = jax.nn.sigmoid(scalar)
        slope = gate * (1.0 - gate)

        def one(j, total):
            at = pl.ds(pl.multiple_of(j * chan, chan), chan)
            value = cot[at, :].astype(jnp.float32)
            dnode[at, :] = value * gate
            return total + value * outs[layer, at, :]

        total = lax.fori_loop(1, coef, one, jnp.zeros((chan, nat), jnp.float32))
        lead = cot[:chan, :].astype(jnp.float32)
        dnode[:chan, :] = lead * (gate + scalar * slope) + total * slope

        def spread(at):
            value = dnode[at, :] / AVG
            high = value.astype(jnp.bfloat16)
            low = (value - high.astype(jnp.float32)).astype(jnp.bfloat16)
            edge_f[at, :] = dot(high, put) + dot(low, put)

        per_coef(spread)

        def write(o, t, cols, total):
            dmix[pl.ds(o * chan + t, 16), cols] = total.astype(jnp.bfloat16)

        mix(edge_f, wig_ref, rows, coef, coef, False, chan, edges, write, early)
        dzero = dmix[:kzero]
        dplus = dmix[kzero : kzero + kone]
        dminus = dmix[kzero + kone :]
        azero = rotated[layer, :kzero]
        aplus = rotated[layer, kzero : kzero + kone]
        aminus = rotated[layer, kzero + kone :]
        store_grads(
            layer,
            (
                lambda: dot(azero, dzero, (1, 1)),
                lambda: dot(aplus, dplus, (1, 1)) + dot(aminus, dminus, (1, 1)),
                lambda: dot(aplus, dminus, (1, 1)) - dot(aminus, dplus, (1, 1)),
            ),
        )
        reduce(layer, 0)
        if last:
            return

        def scaled(value):
            value = value.astype(jnp.bfloat16).astype(jnp.float32)
            scale = rad_ref[layer].astype(jnp.float32)
            parts = value.shape[0] // chan
            return jnp.concatenate(
                [value[k * chan : (k + 1) * chan] * scale for k in range(parts)], axis=0
            )

        small_f[:kzero] = scaled(dot(wzero[...], dzero))
        small_f[kzero : kzero + kone] = scaled(
            dot(wreal[...], dplus) + dot(wimag[...], dminus)
        )
        small_f[kzero + kone :] = scaled(dot(wreal[...], dminus) - dot(wimag[...], dplus))

        def spill(o, t, cols, total):
            edge_g[pl.ds(o * chan + t, 16), cols] = total

        mix(small_f, wig_ref, coef, rows, coef, True, chan, edges, spill, late)

        def collect(at):
            value = edge_g[at, :].astype(jnp.bfloat16)
            back[at, :] = (dnode[at, :] + dot(value, take, (1, 1))).astype(jnp.bfloat16)

        per_coef(collect)

    def step(move, layer, phase):
        return lambda: move(layer, phase)

    forward(
        0, x_ref, False,
        (step(gather, 0, 1), step(gather, 0, 2), step(gather, 0, 3)),
        (step(gather, 1, 1), step(gather, 1, 2)),
    )
    gather(1, 3)
    forward(1, hidden, True, (), ())
    backward(1, cot_ref, False, (), (step(reduce, 1, 1), step(reduce, 1, 2)))
    reduce(1, 3)
    backward(0, back, True, (step(reduce, 1, 4),), ())


def fused_kernel(
    dims, shape, length, own_ref, count_ref, x_ref, cot_ref, wig_ref, rad_ref, src_ref, dst_ref,
    out_ref, full_ref, grad_ref, local_sem, gather_send, gather_recv, *scratch,
):
    zs, ys, xs = dims
    me = place(dims)
    greet(dims, me)
    work, rest = scratch[:13], scratch[13:]
    rows_f = work[0]
    used, rows = length // LANES, own_ref.shape[1]
    gather, gathered = gather_steps(
        dims, me, own_ref, full_ref, local_sem, gather_send, gather_recv
    )
    reduce, reduced = reduce_steps(dims, me, grad_ref, out_ref, rest[0], rest[1:])

    def shards():
        number = 0
        for z in range(zs):
            for y in range(ys):
                for c in range(2):
                    for x in range(xs):
                        yield number, (z, y, c, x)
                        number += 1

    def unpack(layer):
        for number, at in shards():
            rows_f[number * used : number * used + rows, :] = full_ref[(layer,) + at].astype(
                jnp.float32
            )

    def pack(layer):
        for number, at in shards():
            grad_ref[(layer,) + at] = rows_f[number * used : number * used + rows, :].astype(
                jnp.bfloat16
            )

    def moved(layer, phase):
        gather(layer, phase)
        if (layer, phase) == (0, 2):
            gather(1, 0)

    gather(0, 0)
    refs = (count_ref, x_ref, cot_ref, wig_ref, rad_ref, src_ref, dst_ref)
    compute(shape, refs, work, unpack, pack, moved, reduce)
    for phase in range(1, 5):
        reduce(0, phase)
    gathered()
    reduced()


def work_buffers(shape, flat_rows):
    nat, coef, chan, rows, edges = shape
    lone = (rows + 2) // 3
    kzero, kone = lone * chan, (lone - 1) * chan
    wide = coef * chan
    return [
        pltpu.VMEM((flat_rows, LANES), jnp.float32),
        pltpu.VMEM((kzero, kzero), jnp.bfloat16),
        pltpu.VMEM((kone, kone), jnp.bfloat16),
        pltpu.VMEM((kone, kone), jnp.bfloat16),
        pltpu.VMEM((wide, edges), jnp.float32),
        pltpu.VMEM((wide, edges), jnp.float32),
        pltpu.VMEM((2, rows * chan, edges), jnp.bfloat16),
        pltpu.VMEM((rows * chan, edges), jnp.float32),
        pltpu.VMEM((2, wide, nat), jnp.float32),
        pltpu.VMEM((wide, nat), jnp.bfloat16),
        pltpu.VMEM((wide, nat), jnp.bfloat16),
        pltpu.VMEM((wide, nat), jnp.float32),
        pltpu.VMEM((rows * chan, edges), jnp.bfloat16),
    ]


def reduce_scratch(dims, layers, rows):
    zs, ys, xs = dims
    part = rows // PIECES
    most = max(zs, ys, xs, 2) - 1
    count = layers * PIECES
    slots = count * 4 * most
    even, odd = (count + 1) // 2, count // 2
    return (
        [pltpu.VMEM((count, zs, ys, xs, part, LANES), jnp.bfloat16)]
        + reduce_buffers(dims, (("x", "y", even), ("y", "x", odd)), part)
        + [pltpu.SemaphoreType.DMA((slots,)), pltpu.SemaphoreType.DMA((slots,))]
    )


def owned_grads(dims, own, length, inputs, shape, collective_id):
    zs, ys, xs = dims
    layers, rows, _ = own.shape
    most = max(zs, ys, xs, 2) - 1
    slots = layers * PIECES * 4 * most
    spread = (layers, zs, ys, 2, xs, rows, LANES)
    flat_rows = zs * ys * 2 * xs * (length // LANES)
    flat_rows = -(-(flat_rows + rows) // 8) * 8
    vmem = pl.BlockSpec(memory_space=pltpu.VMEM)
    return pl.pallas_call(
        functools.partial(fused_kernel, dims, shape, length),
        out_shape=jax.ShapeDtypeStruct(own.shape, jnp.float32),
        in_specs=[vmem, pl.BlockSpec(memory_space=pltpu.SMEM)] + [vmem] * 6,
        out_specs=vmem,
        scratch_shapes=[
            pltpu.VMEM(spread, jnp.bfloat16),
            pltpu.VMEM(spread, jnp.bfloat16),
            pltpu.SemaphoreType.DMA,
            pltpu.SemaphoreType.DMA((slots,)),
            pltpu.SemaphoreType.DMA((slots,)),
        ]
        + work_buffers(shape, flat_rows)
        + reduce_scratch(dims, layers, rows),
        compiler_params=pltpu.CompilerParams(
            collective_id=collective_id, has_side_effects=True, vmem_limit_bytes=60 << 20
        ),
        name="owned_grads",
    )(own, *inputs)


def device_grads(inputs, flat, shape):
    vmem = pl.BlockSpec(memory_space=pltpu.VMEM)
    return pl.pallas_call(
        functools.partial(compute_kernel, shape),
        out_shape=jax.ShapeDtypeStruct(flat.shape, jnp.bfloat16),
        in_specs=[pl.BlockSpec(memory_space=pltpu.SMEM)] + [vmem] * 7,
        out_specs=vmem,
        scratch_shapes=work_buffers(shape, flat.shape[1]),
        compiler_params=pltpu.CompilerParams(vmem_limit_bytes=56 << 20),
        name="device_grads",
    )(*inputs, flat)


def local(
    dims, node_feats, cotangent, wigner, radial, edge_src, edge_dst, edge_count, params, moment1,
    moment2,
):
    nat, coef, chan = node_feats.shape
    layers, length = params.shape
    zs, ys, xs = dims
    shards = zs * ys * 2 * xs
    block = LANES * 16 * PIECES
    padded = -(-length // block) * block
    rows = padded // LANES
    own = jnp.pad(params.astype(jnp.bfloat16), ((0, 0), (0, padded - length)))
    own = own.reshape(layers, rows, LANES)
    edges = edge_src.shape[0]
    shape = (nat, coef, chan, wigner.shape[0], edges)

    def turned(nodes):
        return jnp.transpose(nodes.reshape(nat, coef * chan))

    inputs = (
        edge_count,
        turned(node_feats),
        turned(cotangent),
        wigner.reshape(-1, edges).astype(jnp.float32),
        jnp.transpose(radial, (0, 2, 1)),
        edge_src[None, :],
        edge_dst[None, :],
    )
    if length % LANES == 0:
        owned = owned_grads(dims, own, length, inputs, shape, 0)
    else:
        full = gather_shards(dims, own, 0).reshape(layers, shards, padded)[:, :, :length]
        full = full.reshape(layers, shards * length // LANES, LANES)
        grad = device_grads(inputs, full, shape).reshape(layers, shards, length)
        grad = jnp.pad(grad, ((0, 0), (0, 0), (0, padded - length)))
        owned = reduce_shards(dims, grad.reshape(layers, zs, ys, 2, xs, rows, LANES), 1)
    grad = owned.reshape(layers, padded)[:, :length]
    new_moment1 = 0.9 * moment1 + 0.1 * grad
    new_moment2 = 0.95 * moment2 + 0.05 * grad * grad
    m_hat = new_moment1 / (1.0 - 0.9**60)
    v_hat = new_moment2 / (1.0 - 0.95**60)
    new_params = params - 0.01 * (m_hat / (jnp.sqrt(v_hat) + 1e-08) + 0.1 * params)
    return (new_params, new_moment1, new_moment2)


def solution(mesh):
    both = ("dp", "node")
    return jax.shard_map(
        functools.partial(local, split_axes(mesh)),
        mesh=mesh,
        in_specs=(
            P(both, None, None),
            P(both, None, None),
            P(None, None, both),
            P(None, both, None),
            P(both),
            P(both),
            P(both),
            P(None, both),
            P(None, both),
            P(None, both),
        ),
        out_specs=(P(None, both), P(None, both), P(None, both)),
        check_vma=False,
    )
```

```python
import functools

import jax
import jax.numpy as jnp
from jax import lax
from jax.experimental import pallas as pl
from jax.experimental.pallas import tpu as pltpu
from jax.sharding import PartitionSpec as P

AVG = 10
LANES = 128
PIECES = 3
LINK = jnp.bfloat16


def split_axes(mesh):
    rest = mesh.shape["dp"] // 2
    y = 1
    while y * y * 4 <= rest and rest % (y * 2) == 0:
        y *= 2
    return rest // y, y, mesh.shape["node"]


def place(dims):
    zs, ys, xs = dims
    dp = lax.axis_index("dp")
    x = lax.axis_index("node")
    core = lax.rem(dp, 2)
    y = lax.rem(dp // 2, ys)
    z = dp // (2 * ys)
    return {"z": z, "y": y, "c": core, "x": x}


def device(dims, at):
    return {"dp": (at["z"] * dims[1] + at["y"]) * 2 + at["c"], "node": at["x"]}


def peer_of(dims, me, axis, step):
    size = {"z": dims[0], "y": dims[1], "c": 2, "x": dims[2]}[axis]
    other = dict(me)
    other[axis] = lax.rem(me[axis] + step, size)
    return other


def size_of(dims, axis):
    return {"z": dims[0], "y": dims[1], "c": 2, "x": dims[2]}[axis]


def greet(dims, me):
    barrier = pltpu.get_barrier_semaphore()
    count = 0
    for axis in "zyxc":
        for step in range(1, size_of(dims, axis)):
            pl.semaphore_signal(
                barrier,
                inc=1,
                device_id=device(dims, peer_of(dims, me, axis, step)),
                device_id_type=pl.DeviceIdType.MESH,
            )
            count += 1
    pl.semaphore_wait(barrier, count)


def gather_steps(dims, me, own_ref, out_ref, local_sem, send_sem, recv_sem):
    layers, rows = own_ref.shape[0], own_ref.shape[1]
    part = rows // PIECES
    mine = pltpu.make_async_copy(
        own_ref, out_ref.at[:, me["z"], me["y"], me["c"], me["x"]], local_sem
    )
    mine.start()
    most = max(size_of(dims, a) for a in "zyxc") - 1
    started = {}
    state = {"mine": True}

    def view(ref, layer, piece, spans, at):
        index = [layer]
        for axis in "zycx":
            index.append(slice(None) if axis in spans else at[axis])
        index.append(pl.ds(piece * part, part))
        return ref.at[tuple(index)]

    def advance(layer, phase):
        for piece in range(PIECES):
            number = layer * PIECES + piece
            order = ("yxzc", "zyxc", "zxyc")[piece % 3]
            if phase:
                for copy in started[number, phase - 1]:
                    copy.wait_recv()
                if state["mine"]:
                    mine.wait()
                    state["mine"] = False
            if phase == 4:
                continue
            axis, spans = order[phase], order[:phase]
            copies = []
            for step in range(1, size_of(dims, axis)):
                if phase == 0:
                    src = own_ref.at[layer, pl.ds(piece * part, part)]
                else:
                    src = view(out_ref, layer, piece, spans, me)
                slot = (number * 4 + phase) * most + step - 1
                copy = pltpu.make_async_remote_copy(
                    src_ref=src,
                    dst_ref=view(out_ref, layer, piece, spans, me),
                    send_sem=send_sem.at[slot],
                    recv_sem=recv_sem.at[slot],
                    device_id=device(dims, peer_of(dims, me, axis, step)),
                    device_id_type=pl.DeviceIdType.MESH,
                )
                copy.start()
                copies.append(copy)
            started[number, phase] = copies

    def finish():
        for copies in started.values():
            for copy in copies:
                copy.wait_send()

    return advance, finish


def gather_kernel(dims, own_ref, out_ref, local_sem, send_sem, recv_sem):
    me = place(dims)
    greet(dims, me)
    advance, finish = gather_steps(dims, me, own_ref, out_ref, local_sem, send_sem, recv_sem)
    for phase in range(5):
        for layer in range(own_ref.shape[0]):
            advance(layer, phase)
    finish()


def gather_shards(dims, own, collective_id):
    layers, rows, lanes = own.shape
    zs, ys, xs = dims
    most = max(zs, ys, xs, 2) - 1
    slots = layers * PIECES * 4 * most
    return pl.pallas_call(
        functools.partial(gather_kernel, dims),
        out_shape=jax.ShapeDtypeStruct((layers, zs, ys, 2, xs, rows, lanes), own.dtype),
        in_specs=[pl.BlockSpec(memory_space=pltpu.VMEM)],
        out_specs=pl.BlockSpec(memory_space=pltpu.VMEM),
        scratch_shapes=[
            pltpu.SemaphoreType.DMA,
            pltpu.SemaphoreType.DMA((slots,)),
            pltpu.SemaphoreType.DMA((slots,)),
        ],
        compiler_params=pltpu.CompilerParams(
            collective_id=collective_id, has_side_effects=True, vmem_limit_bytes=48 << 20
        ),
        name="gather_shards",
    )(own)


def reduce_buffers(dims, pairs, part):
    zs = dims[0]
    buffers = []
    for first, second, count in pairs:
        n1, n2 = size_of(dims, first), size_of(dims, second)
        buffers += [
            pltpu.VMEM((count, zs, n2, part, LANES), jnp.float32),
            pltpu.VMEM((count, n1 - 1, zs, n2, part, LANES), LINK),
            pltpu.VMEM((count, n1 - 1, zs, n2, part, LANES), LINK),
            pltpu.VMEM((count, zs, part, LANES), jnp.float32),
            pltpu.VMEM((count, n2 - 1, zs, part, LANES), LINK),
            pltpu.VMEM((count, n2 - 1, zs, part, LANES), LINK),
            pltpu.VMEM((count, part, LANES), jnp.float32),
            pltpu.VMEM((count, zs - 1, part, LANES), LINK),
            pltpu.VMEM((count, zs - 1, part, LANES), LINK),
        ]
    return buffers


def reduce_items(layers):
    items = []
    for layer in reversed(range(layers)):
        for piece in range(PIECES):
            number = len(items)
            items.append((layer, piece, number % 2, number // 2))
    return items


def reduce_steps(dims, me, grad_ref, out_ref, pair_buf, scratch):
    zs = dims[0]
    buffers = (scratch[:9], scratch[9:18])
    send_sem, recv_sem = scratch[18:20]
    layers, rows = out_ref.shape[0], out_ref.shape[1]
    part = rows // PIECES
    items = reduce_items(layers)
    most = max(size_of(dims, a) for a in "zyxc") - 1
    pending = []

    def send(number, phase, step, axis, src, dst):
        slot = (number * 4 + phase) * most + step - 1
        copy = pltpu.make_async_remote_copy(
            src_ref=src,
            dst_ref=dst,
            send_sem=send_sem.at[slot],
            recv_sem=recv_sem.at[slot],
            device_id=device(dims, peer_of(dims, me, axis, step)),
            device_id_type=pl.DeviceIdType.MESH,
        )
        copy.start()
        pending.append(copy)
        return copy

    def f32(value):
        return value.astype(jnp.float32)

    waits = {}

    def advance(wanted, now):
        phase = now - 1
        for number, (layer, piece, kind, place_in) in enumerate(items):
            if layer != wanted:
                continue
            if now == 0:
                waits[number] = [
                    send(
                        number, 0, 1, "c",
                        grad_ref.at[layer, :, :, 1 - me["c"], :, pl.ds(piece * part, part)],
                        pair_buf.at[number],
                    )
                ]
                continue
            span = pl.ds(piece * part, part)
            acc1, send1, recv1, acc2, send2, recv2, acc3, send3, recv3 = (
                buf.at[place_in] for buf in buffers[kind]
            )
            first, second = ("x", "y") if kind == 0 else ("y", "x")
            n1, n2 = size_of(dims, first), size_of(dims, second)
            for copy in waits[number]:
                copy.wait_recv()
            copies = []
            if phase == 0:
                for step in list(range(1, n1)) + [0]:
                    k1 = lax.rem(me[first] + step, n1)

                    def one(i, carry, step=step, k1=k1):
                        z, k2 = i // n2, lax.rem(i, n2)
                        y, x = (k2, k1) if kind == 0 else (k1, k2)
                        total = f32(grad_ref[layer, z, y, me["c"], x, span]) + f32(
                            pair_buf[number, z, y, x]
                        )
                        if step:
                            send1[step - 1, z, k2] = total.astype(LINK)
                        else:
                            acc1[z, k2] = total
                        return carry

                    lax.fori_loop(0, zs * n2, one, 0)
                    if step:
                        copies.append(
                            send(number, 1, step, first, send1.at[step - 1], recv1.at[step - 1])
                        )
            elif phase == 1:
                for step in list(range(1, n2)) + [0]:
                    k2 = lax.rem(me[second] + step, n2)

                    def one(z, carry, step=step, k2=k2):
                        total = acc1[z, k2]
                        for e in range(n1 - 1):
                            total = total + f32(recv1[e, z, k2])
                        if step:
                            send2[step - 1, z] = total.astype(LINK)
                        else:
                            acc2[z] = total
                        return carry

                    lax.fori_loop(0, zs, one, 0)
                    if step:
                        copies.append(
                            send(number, 2, step, second, send2.at[step - 1], recv2.at[step - 1])
                        )
            elif phase == 2:
                for step in list(range(1, zs)) + [0]:
                    z = lax.rem(me["z"] + step, zs)
                    total = acc2[z]
                    for e in range(n2 - 1):
                        total = total + f32(recv2[e, z])
                    if step:
                        send3[step - 1] = total.astype(LINK)
                        copies.append(
                            send(number, 3, step, "z", send3.at[step - 1], recv3.at[step - 1])
                        )
                    else:
                        acc3[...] = total
            else:
                total = acc3[...]
                for e in range(zs - 1):
                    total = total + f32(recv3[e])
                out_ref[layer, span] = total
            waits[number] = copies

    def finish():
        for copy in pending:
            copy.wait_send()

    return advance, finish


def reduce_kernel(dims, grad_ref, out_ref, pair_buf, *scratch):
    me = place(dims)
    greet(dims, me)
    advance, finish = reduce_steps(dims, me, grad_ref, out_ref, pair_buf, scratch)
    for phase in range(5):
        for layer in reversed(range(out_ref.shape[0])):
            advance(layer, phase)
    finish()


def reduce_shards(dims, grad, collective_id):
    layers, _, _, _, _, rows, lanes = grad.shape
    return pl.pallas_call(
        functools.partial(reduce_kernel, dims),
        out_shape=jax.ShapeDtypeStruct((layers, rows, lanes), jnp.float32),
        in_specs=[pl.BlockSpec(memory_space=pltpu.VMEM)],
        out_specs=pl.BlockSpec(memory_space=pltpu.VMEM),
        scratch_shapes=reduce_scratch(dims, layers, rows),
        compiler_params=pltpu.CompilerParams(
            collective_id=collective_id, has_side_effects=True, vmem_limit_bytes=48 << 20
        ),
        name="reduce_shards",
    )(grad)


def mix(source, wig, outputs, inputs, coef, transposed, chan, edges, write, hooks=()):
    tall = 16
    wide = LANES if edges % LANES == 0 else edges
    across = edges // wide

    def one(number, carry):
        t, h = number // across, lax.rem(number, across)
        cols = pl.ds(pl.multiple_of(h * wide, wide), wide)
        tiles = [
            source[pl.ds(pl.multiple_of(i * chan + t * tall, tall), tall), cols]
            for i in range(inputs)
        ]
        for o in range(outputs):
            total = None
            for i in range(inputs):
                row = i * coef + o if transposed else o * coef + i
                term = wig[pl.ds(row, 1), cols] * tiles[i]
                total = term if total is None else total + term
            write(o, pl.multiple_of(t * tall, tall), cols, total)
        return carry

    total = (chan // tall) * across
    spans = len(hooks) + 1
    for n in range(spans):
        lax.fori_loop(n * total // spans, (n + 1) * total // spans, one, 0)
        if n < len(hooks):
            hooks[n]()


def dot(a, b, over=(1, 0)):
    return lax.dot_general(
        a, b, (((over[0],), (over[1],)), ((), ())), preferred_element_type=jnp.float32
    )


def compute_kernel(
    shape, count_ref, x_ref, cot_ref, wig_ref, rad_ref, src_ref, dst_ref, flat_ref, grad_ref,
    *scratch,
):
    rows_f = scratch[0]

    def unpack(layer):
        rows_f[...] = flat_ref[layer].astype(jnp.float32)

    def pack(layer):
        grad_ref[layer] = rows_f[...].astype(jnp.bfloat16)

    refs = (count_ref, x_ref, cot_ref, wig_ref, rad_ref, src_ref, dst_ref)
    compute(shape, refs, scratch, unpack, pack, lambda *step: None, lambda *step: None)


def compute(shape, refs, scratch, unpack, pack, gather, reduce):
    count_ref, x_ref, cot_ref, wig_ref, rad_ref, src_ref, dst_ref = refs
    (rows_f, wzero, wreal, wimag, edge_f, edge_g, rotated, small_f, outs, hidden, back, dnode, dmix) = scratch
    nat, coef, chan, rows, edges = shape
    lone = (rows + 2) // 3
    kzero, kone = lone * chan, (lone - 1) * chan
    atoms = lax.broadcasted_iota(jnp.int32, (nat, edges), 0)
    slots = lax.broadcasted_iota(jnp.int32, (nat, edges), 1)
    take = (src_ref[...] == atoms).astype(jnp.float32).astype(jnp.bfloat16)
    live = (dst_ref[...] == atoms) & (slots < count_ref[0])
    put = live.astype(jnp.float32).astype(jnp.bfloat16)

    def per_coef(body):
        def one(j, carry):
            body(pl.ds(pl.multiple_of(j * chan, chan), chan))
            return carry

        lax.fori_loop(0, coef, one, 0)

    def blocks():
        cut = kzero * kzero // LANES
        step = kone * kone // LANES
        return ((wzero, 0, kzero), (wreal, cut, kone), (wimag, cut + step, kone))

    def load_weights(layer):
        unpack(layer)
        for ref, start, size in blocks():
            per = size // LANES
            for c in range(per):
                ref[:, c * LANES : (c + 1) * LANES] = rows_f[
                    pl.ds(start + c, size, stride=per), :
                ].astype(jnp.bfloat16)

    def store_grads(layer, grads):
        for (_, start, size), grad in zip(blocks(), grads):
            per = size // LANES
            value = grad()
            for c in range(per):
                rows_f[pl.ds(start + c, size, stride=per), :] = value[
                    :, c * LANES : (c + 1) * LANES
                ]
        pack(layer)

    def forward(layer, node, last, early, late):
        def pick(at):
            edge_f[at, :] = dot(node[at, :], take)

        per_coef(pick)

        def write(o, t, cols, total):
            scaled = total * rad_ref[layer, pl.ds(t, 16), cols].astype(jnp.float32)
            rotated[layer, pl.ds(o * chan + t, 16), cols] = scaled.astype(jnp.bfloat16)

        mix(edge_f, wig_ref, rows, coef, coef, False, chan, edges, write, early)
        gather(layer, 4)
        load_weights(layer)
        azero = rotated[layer, :kzero]
        aplus = rotated[layer, kzero : kzero + kone]
        aminus = rotated[layer, kzero + kone :]

        def rounded(value):
            return value.astype(jnp.bfloat16).astype(jnp.float32)

        small_f[:kzero] = rounded(dot(wzero[...], azero, (0, 0)))
        small_f[kzero : kzero + kone] = rounded(
            dot(wreal[...], aplus, (0, 0)) - dot(wimag[...], aminus, (0, 0))
        )
        small_f[kzero + kone :] = rounded(
            dot(wimag[...], aplus, (0, 0)) + dot(wreal[...], aminus, (0, 0))
        )

        def message(o, t, cols, total):
            edge_g[pl.ds(o * chan + t, 16), cols] = total

        mix(small_f, wig_ref, coef, rows, coef, True, chan, edges, message, late)

        def gathered(at):
            value = edge_g[at, :]
            high = value.astype(jnp.bfloat16)
            low = (value - high.astype(jnp.float32)).astype(jnp.bfloat16)
            total = dot(high, put, (1, 1)) + dot(low, put, (1, 1))
            outs[layer, at, :] = node[at, :].astype(jnp.float32) + total / AVG

        per_coef(gathered)
        if last:
            return
        gate = jax.nn.sigmoid(outs[layer, :chan, :])

        def activate(at):
            hidden[at, :] = (outs[layer, at, :] * gate).astype(jnp.bfloat16)

        per_coef(activate)

    def backward(layer, cot, last, early, late):
        scalar = outs[layer, :chan, :]
        gate = jax.nn.sigmoid(scalar)
        slope = gate * (1.0 - gate)

        def one(j, total):
            at = pl.ds(pl.multiple_of(j * chan, chan), chan)
            value = cot[at, :].astype(jnp.float32)
            dnode[at, :] = value * gate
            return total + value * outs[layer, at, :]

        total = lax.fori_loop(1, coef, one, jnp.zeros((chan, nat), jnp.float32))
        lead = cot[:chan, :].astype(jnp.float32)
        dnode[:chan, :] = lead * (gate + scalar * slope) + total * slope

        def spread(at):
            value = dnode[at, :] / AVG
            high = value.astype(jnp.bfloat16)
            low = (value - high.astype(jnp.float32)).astype(jnp.bfloat16)
            edge_f[at, :] = dot(high, put) + dot(low, put)

        per_coef(spread)

        def write(o, t, cols, total):
            dmix[pl.ds(o * chan + t, 16), cols] = total.astype(jnp.bfloat16)

        mix(edge_f, wig_ref, rows, coef, coef, False, chan, edges, write, early)
        dzero = dmix[:kzero]
        dplus = dmix[kzero : kzero + kone]
        dminus = dmix[kzero + kone :]
        azero = rotated[layer, :kzero]
        aplus = rotated[layer, kzero : kzero + kone]
        aminus = rotated[layer, kzero + kone :]
        store_grads(
            layer,
            (
                lambda: dot(azero, dzero, (1, 1)),
                lambda: dot(aplus, dplus, (1, 1)) + dot(aminus, dminus, (1, 1)),
                lambda: dot(aplus, dminus, (1, 1)) - dot(aminus, dplus, (1, 1)),
            ),
        )
        reduce(layer, 0)
        if last:
            return

        def scaled(value):
            value = value.astype(jnp.bfloat16).astype(jnp.float32)
            scale = rad_ref[layer].astype(jnp.float32)
            parts = value.shape[0] // chan
            return jnp.concatenate(
                [value[k * chan : (k + 1) * chan] * scale for k in range(parts)], axis=0
            )

        small_f[:kzero] = scaled(dot(wzero[...], dzero))
        small_f[kzero : kzero + kone] = scaled(
            dot(wreal[...], dplus) + dot(wimag[...], dminus)
        )
        small_f[kzero + kone :] = scaled(dot(wreal[...], dminus) - dot(wimag[...], dplus))

        def spill(o, t, cols, total):
            edge_g[pl.ds(o * chan + t, 16), cols] = total

        mix(small_f, wig_ref, coef, rows, coef, True, chan, edges, spill, late)

        def collect(at):
            value = edge_g[at, :].astype(jnp.bfloat16)
            back[at, :] = (dnode[at, :] + dot(value, take, (1, 1))).astype(jnp.bfloat16)

        per_coef(collect)

    def step(move, layer, phase):
        return lambda: move(layer, phase)

    forward(
        0, x_ref, False,
        (step(gather, 0, 1), step(gather, 0, 2), step(gather, 0, 3)),
        (step(gather, 1, 1), step(gather, 1, 2)),
    )
    gather(1, 3)
    forward(1, hidden, True, (), ())
    backward(1, cot_ref, False, (), (step(reduce, 1, 1), step(reduce, 1, 2)))
    reduce(1, 3)
    backward(0, back, True, (step(reduce, 1, 4),), ())


def fused_kernel(
    dims, shape, length, own_ref, count_ref, x_ref, cot_ref, wig_ref, rad_ref, src_ref, dst_ref,
    out_ref, full_ref, grad_ref, local_sem, gather_send, gather_recv, *scratch,
):
    zs, ys, xs = dims
    me = place(dims)
    greet(dims, me)
    work, rest = scratch[:13], scratch[13:]
    rows_f = work[0]
    used, rows = length // LANES, own_ref.shape[1]
    gather, gathered = gather_steps(
        dims, me, own_ref, full_ref, local_sem, gather_send, gather_recv
    )
    reduce, reduced = reduce_steps(dims, me, grad_ref, out_ref, rest[0], rest[1:])

    def shards():
        number = 0
        for z in range(zs):
            for y in range(ys):
                for c in range(2):
                    for x in range(xs):
                        yield number, (z, y, c, x)
                        number += 1

    def unpack(layer):
        for number, at in shards():
            rows_f[number * used : number * used + rows, :] = full_ref[(layer,) + at].astype(
                jnp.float32
            )

    def pack(layer):
        for number, at in shards():
            grad_ref[(layer,) + at] = rows_f[number * used : number * used + rows, :].astype(
                jnp.bfloat16
            )

    def moved(layer, phase):
        gather(layer, phase)
        if (layer, phase) == (0, 2):
            gather(1, 0)

    gather(0, 0)
    refs = (count_ref, x_ref, cot_ref, wig_ref, rad_ref, src_ref, dst_ref)
    compute(shape, refs, work, unpack, pack, moved, reduce)
    for phase in range(1, 5):
        reduce(0, phase)
    gathered()
    reduced()


def work_buffers(shape, flat_rows):
    nat, coef, chan, rows, edges = shape
    lone = (rows + 2) // 3
    kzero, kone = lone * chan, (lone - 1) * chan
    wide = coef * chan
    return [
        pltpu.VMEM((flat_rows, LANES), jnp.float32),
        pltpu.VMEM((kzero, kzero), jnp.bfloat16),
        pltpu.VMEM((kone, kone), jnp.bfloat16),
        pltpu.VMEM((kone, kone), jnp.bfloat16),
        pltpu.VMEM((wide, edges), jnp.float32),
        pltpu.VMEM((wide, edges), jnp.float32),
        pltpu.VMEM((2, rows * chan, edges), jnp.bfloat16),
        pltpu.VMEM((rows * chan, edges), jnp.float32),
        pltpu.VMEM((2, wide, nat), jnp.float32),
        pltpu.VMEM((wide, nat), jnp.bfloat16),
        pltpu.VMEM((wide, nat), jnp.bfloat16),
        pltpu.VMEM((wide, nat), jnp.float32),
        pltpu.VMEM((rows * chan, edges), jnp.bfloat16),
    ]


def reduce_scratch(dims, layers, rows):
    zs, ys, xs = dims
    part = rows // PIECES
    most = max(zs, ys, xs, 2) - 1
    count = layers * PIECES
    slots = count * 4 * most
    even, odd = (count + 1) // 2, count // 2
    return (
        [pltpu.VMEM((count, zs, ys, xs, part, LANES), jnp.bfloat16)]
        + reduce_buffers(dims, (("x", "y", even), ("y", "x", odd)), part)
        + [pltpu.SemaphoreType.DMA((slots,)), pltpu.SemaphoreType.DMA((slots,))]
    )


def owned_grads(dims, own, length, inputs, shape, collective_id):
    zs, ys, xs = dims
    layers, rows, _ = own.shape
    most = max(zs, ys, xs, 2) - 1
    slots = layers * PIECES * 4 * most
    spread = (layers, zs, ys, 2, xs, rows, LANES)
    flat_rows = zs * ys * 2 * xs * (length // LANES)
    flat_rows = -(-(flat_rows + rows) // 8) * 8
    vmem = pl.BlockSpec(memory_space=pltpu.VMEM)
    return pl.pallas_call(
        functools.partial(fused_kernel, dims, shape, length),
        out_shape=jax.ShapeDtypeStruct(own.shape, jnp.float32),
        in_specs=[vmem, pl.BlockSpec(memory_space=pltpu.SMEM)] + [vmem] * 6,
        out_specs=vmem,
        scratch_shapes=[
            pltpu.VMEM(spread, jnp.bfloat16),
            pltpu.VMEM(spread, jnp.bfloat16),
            pltpu.SemaphoreType.DMA,
            pltpu.SemaphoreType.DMA((slots,)),
            pltpu.SemaphoreType.DMA((slots,)),
        ]
        + work_buffers(shape, flat_rows)
        + reduce_scratch(dims, layers, rows),
        compiler_params=pltpu.CompilerParams(
            collective_id=collective_id, has_side_effects=True, vmem_limit_bytes=60 << 20
        ),
        name="owned_grads",
    )(own, *inputs)


def device_grads(inputs, flat, shape):
    vmem = pl.BlockSpec(memory_space=pltpu.VMEM)
    return pl.pallas_call(
        functools.partial(compute_kernel, shape),
        out_shape=jax.ShapeDtypeStruct(flat.shape, jnp.bfloat16),
        in_specs=[pl.BlockSpec(memory_space=pltpu.SMEM)] + [vmem] * 7,
        out_specs=vmem,
        scratch_shapes=work_buffers(shape, flat.shape[1]),
        compiler_params=pltpu.CompilerParams(vmem_limit_bytes=56 << 20),
        name="device_grads",
    )(*inputs, flat)


def local(
    dims, node_feats, cotangent, wigner, radial, edge_src, edge_dst, edge_count, params, moment1,
    moment2,
):
    nat, coef, chan = node_feats.shape
    layers, length = params.shape
    zs, ys, xs = dims
    shards = zs * ys * 2 * xs
    block = LANES * 16 * PIECES
    padded = -(-length // block) * block
    rows = padded // LANES
    own = jnp.pad(params.astype(jnp.bfloat16), ((0, 0), (0, padded - length)))
    own = own.reshape(layers, rows, LANES)
    edges = edge_src.shape[0]
    shape = (nat, coef, chan, wigner.shape[0], edges)

    def turned(nodes):
        return jnp.transpose(nodes.reshape(nat, coef * chan))

    inputs = (
        edge_count,
        turned(node_feats),
        turned(cotangent),
        wigner.reshape(-1, edges).astype(jnp.float32),
        jnp.transpose(radial, (0, 2, 1)),
        edge_src[None, :],
        edge_dst[None, :],
    )
    if length % LANES == 0:
        owned = owned_grads(dims, own, length, inputs, shape, 0)
    else:
        full = gather_shards(dims, own, 0).reshape(layers, shards, padded)[:, :, :length]
        full = full.reshape(layers, shards * length // LANES, LANES)
        grad = device_grads(inputs, full, shape).reshape(layers, shards, length)
        grad = jnp.pad(grad, ((0, 0), (0, 0), (0, padded - length)))
        owned = reduce_shards(dims, grad.reshape(layers, zs, ys, 2, xs, rows, LANES), 1)
    grad = owned.reshape(layers, padded)[:, :length]
    new_moment1 = 0.9 * moment1 + 0.1 * grad
    new_moment2 = 0.95 * moment2 + 0.05 * grad * grad
    m_hat = new_moment1 / (1.0 - 0.9**60)
    v_hat = new_moment2 / (1.0 - 0.95**60)
    new_params = params - 0.01 * (m_hat / (jnp.sqrt(v_hat) + 1e-08) + 0.1 * params)
    return (new_params, new_moment1, new_moment2)


def solution(mesh):
    both = ("dp", "node")
    return jax.shard_map(
        functools.partial(local, split_axes(mesh)),
        mesh=mesh,
        in_specs=(
            P(both, None, None),
            P(both, None, None),
            P(None, None, both),
            P(None, both, None),
            P(both),
            P(both),
            P(both),
            P(None, both),
            P(None, both),
            P(None, both),
        ),
        out_specs=(P(None, both), P(None, both), P(None, both)),
        check_vma=False,
    )
```
